512 devices in a mesh: segment: 4 (over x), expert: 64 (over y, z), dp: 2 (over core).
Axes of the slice: x: 4, y: 4, z: 16, core: 2. Of those that a mesh axis runs over, the one named last changes fastest.
Arguments:
- act_in: bfloat16 [4, 14336, 2048], P('segment', ('expert', 'dp')), may hold values from -6 to 6
- stash_in: bfloat16 [4, 14336, 2048], P('segment', ('expert', 'dp')), may hold values from -6 to 6
- grad_in: bfloat16 [4, 14336, 2048], P('segment', ('expert', 'dp')), may hold values from -6 to 6
- route_a: int32 [4, 14336, 2], P('segment', ('expert', 'dp')), may hold values from 0 to 31, all different within a row; in each aligned block of 112 rows (0 to 111, 112 to 223, ..., all dimensions but the last counted through in order) at most 8 rows name the same one
- route_b: int32 [4, 14336, 2], P('segment', ('expert', 'dp')), may hold values from 0 to 31, all different within a row; in each aligned block of 112 rows (0 to 111, 112 to 223, ..., all dimensions but the last counted through in order) at most 8 rows name the same one
- norm_gain: float32 [4, 2048], P('segment'), may hold values from 0.5 to 1.5
- router: bfloat16 [4, 32, 2048], P('segment'), may hold values from -0.5 to 0.5
- gate_weight: bfloat16 [4, 64, 352, 2048], P('segment', 'expert', 'dp'), may hold values from -0.125 to 0.125
- up_weight: bfloat16 [4, 64, 352, 2048], P('segment', 'expert', 'dp'), may hold values from -0.125 to 0.125
- down_weight: bfloat16 [4, 64, 352, 2048], P('segment', 'expert', 'dp'), may hold values from -0.21875 to 0.21875
Outputs:
- next_act: bfloat16 [4, 14336, 2048], P('segment', ('expert', 'dp'))
- prev_grad: bfloat16 [4, 14336, 2048], P('segment', ('expert', 'dp'))
- router_grad: float32 [4, 32, 2048], P('segment')
- gain_grad: float32 [4, 2048], P('segment')
The draws below stay inside these ranges and needn't reach their ends.
Inputs may be any that keep to these rules, and one draw needn't show every extreme that they name: `route_a`: each row names two different experts. In each aligned block of 112 rows (the tokens of one device) no expert is named more than 8 times, a bound that some block reaches in every draw. `route_b`: as route_a.
All inputs are finite; a program needn't handle non-finite values.
Results may differ from the reference program's by a relative error of at most 0.011.
Values may be sent and summed in bfloat16 or wider, within the bound.
A program may use at most 64 MiB of HBM per device.

```python
import math
import jax
import jax.numpy as jnp
import numpy as np
from jax import lax

D = 2048
FF = 704
TOK = 112
EXPERTS = 32
MOST = 8
TOKENS = 14336
N_SEGMENT = 4
N_EXPERT = 64
N_DP = 2


def steps_of(stream_key, shape, shards, low, high):
    def one(position, shards_of):
        heights = jax.random.uniform(jax.random.fold_in(jax.random.fold_in(stream_key, 6), position), (shards_of,), jnp.float32, low / len(shards), high / len(shards))
        return jnp.repeat(jnp.exp(heights), shape[position] // shards_of).reshape((-1,) + (1,) * (len(shape) - position - 1))

    level = one(*shards[0])
    for cut in shards[1:]:
        level = level * one(*cut)
    return level


def deal_out(own_key, own, number, rows, number_of, top, limit, skew):
    sequence = jax.random.permutation(own_key, number_of)
    crowded, common = load_shares(number_of, rows * top, limit, skew, True), load_shares(number_of, rows * top, limit, skew, False)
    places = jnp.arange(number_of)

    def named(lengths, offset_by):
        used = int((lengths > 0).sum())
        fixed = max(1, used // 4)
        moved = fixed + (places - fixed + offset_by * (used - fixed)) % max(1, number_of - fixed)
        return jnp.zeros((number_of,), jnp.int32).at[sequence[jnp.where(places < fixed, places, moved)]].set(jnp.asarray(lengths, jnp.int32))

    lengths = jnp.where(number % 4 == 0, named(crowded, number // 4), named(common, number - number // 4 - 1))
    mixed = jax.random.permutation(jax.random.fold_in(own, 3), number_of)
    donor, receiver = mixed[0:number_of // 2 * 2:2], mixed[1:number_of // 2 * 2:2]
    room = jnp.minimum(lengths[donor] - 1, limit - lengths[receiver]) // 2
    room = jnp.where((donor == sequence[0]) | (receiver == sequence[0]) | (lengths[receiver] == 0), 0, jnp.maximum(room, 0))
    moved = jax.random.randint(jax.random.fold_in(own, 4), (number_of // 2,), 0, 1 << 20) % (room + 1)
    lengths = lengths.at[donor].add(-moved).at[receiver].add(moved)
    labels = jnp.searchsorted(jnp.cumsum(lengths), jnp.arange(rows * top), side="right").astype(jnp.int32)
    table = labels.reshape(top, rows).T
    table = table[jax.random.permutation(jax.random.fold_in(own, 1), rows)]
    offset_by = jax.random.randint(jax.random.fold_in(own, 2), (rows, 1), 0, top)
    return jnp.take_along_axis(table, (jnp.arange(top)[None, :] + offset_by) % top, axis=1)


def load_shares(count, total, reach, slope, full):
    loads = [(1 << 20) // math.isqrt(standing ** slope) + 1 for standing in range(1, count + 1)]
    largest = reach if full else min(reach, max(-(-total // count), total * loads[0] // sum(loads)))
    least = 1 if total - largest >= count - 1 else 0
    counts, surplus = [largest] + [least] * (count - 1), total - largest - least * (count - 1)
    while surplus > 0:
        movable = [i for i in range(1, count) if counts[i] < largest] or [i for i in range(1, count) if counts[i] < reach]
        mass, budget = sum([loads[i] for i in movable]), surplus
        for i in movable:
            addition = min(reach - counts[i], max(1, budget * loads[i] // mass), surplus)
            counts[i] = counts[i] + addition
            surplus = surplus - addition
    return np.array(counts)


def bell_draw(own_key, extent, spread, reach, shards=(), held_as=jnp.bfloat16):
    array = spread * jax.random.normal(own_key, extent, jnp.float32)
    if shards:
        array = array * steps_of(own_key, extent, shards, -0.22, 0.18)
    return jnp.clip(array, -reach, reach).astype(held_as)


def setup_inputs(seed: int = 0) -> dict:
    keys = jax.random.split(jax.random.key(seed), 11)
    act_in = bell_draw(keys[0], (N_SEGMENT, TOKENS, D), 1.0, 6.0, ((0, 4), (1, 128)))
    stash_in = bell_draw(keys[1], (N_SEGMENT, TOKENS, D), 1.0, 6.0, ((0, 4), (1, 128)))
    grad_in = bell_draw(keys[2], (N_SEGMENT, TOKENS, D), 1.0, 6.0, ((0, 4), (1, 128)))
    route_a_keys = jax.random.split(jax.random.fold_in(keys[3], 1), N_SEGMENT * TOKENS // TOK)
    route_a_turns = jax.random.permutation(jax.random.fold_in(keys[3], 3), N_SEGMENT * TOKENS // TOK)
    route_a = jax.vmap(lambda own, number: deal_out(jax.random.fold_in(keys[3], 2), own, number, TOK, EXPERTS, 2, MOST, 2))(route_a_keys, route_a_turns).reshape((N_SEGMENT, TOKENS, 2))
    route_b_keys = jax.random.split(jax.random.fold_in(keys[4], 1), N_SEGMENT * TOKENS // TOK)
    route_b_turns = jax.random.permutation(jax.random.fold_in(keys[4], 3), N_SEGMENT * TOKENS // TOK)
    route_b = jax.vmap(lambda own, number: deal_out(jax.random.fold_in(keys[4], 2), own, number, TOK, EXPERTS, 2, MOST, 2))(route_b_keys, route_b_turns).reshape((N_SEGMENT, TOKENS, 2))
    norm_gain = jnp.clip(1.0 + 0.1 * jax.random.normal(keys[5], (N_SEGMENT, D), jnp.float32), 0.5, 1.5)
    router = bell_draw(keys[6], (N_SEGMENT, EXPERTS, D), (D // 16) ** -0.5, 0.5, ((0, 4),))
    gate_weight = bell_draw(keys[7], (N_SEGMENT, N_EXPERT, FF // 2, D), D ** -0.5, 0.125, ((0, 4), (1, 64), (2, 2)))
    up_weight = bell_draw(keys[8], (N_SEGMENT, N_EXPERT, FF // 2, D), D ** -0.5, 0.125, ((0, 4), (1, 64), (2, 2)))
    down_weight = bell_draw(keys[9], (N_SEGMENT, N_EXPERT, FF // 2, D), FF ** -0.5, 0.21875, ((0, 4), (1, 64), (2, 2)))
    return dict(act_in=act_in, stash_in=stash_in, grad_in=grad_in, route_a=route_a, route_b=route_b, norm_gain=norm_gain, router=router, gate_weight=gate_weight, up_weight=up_weight, down_weight=down_weight)


EPS = 1e-06

def prepare(x_block, route, gain, router_w):
    x_float = x_block.astype(jnp.float32)
    inv_rms = lax.rsqrt(lax.optimization_barrier(jnp.mean(x_float * x_float, -1, keepdims=True)) + EPS)
    normed = (x_float * inv_rms * gain[None, :]).astype(jnp.bfloat16)
    logits = jnp.dot(normed, router_w.T, preferred_element_type=jnp.float32)
    chosen_mask = route[:, :, None] == jnp.arange(EXPERTS, dtype=jnp.int32)[None, None, :]
    chosen = lax.optimization_barrier(jnp.sum(jnp.where(chosen_mask, logits[:, None, :], 0.0), -1))
    weight_one = jax.nn.sigmoid(chosen[:, 0] - chosen[:, 1])
    weight_two = jax.nn.sigmoid(chosen[:, 1] - chosen[:, 0])
    return (x_float, inv_rms, normed, chosen_mask, weight_one, weight_two)

def expert_table(route):
    blocks = N_EXPERT * N_DP
    pair_count = TOKENS * 2
    expert_ids = route.reshape(blocks, 2 * TOK)
    onehot = (expert_ids[:, :, None] == jnp.arange(EXPERTS, dtype=jnp.int32)[None, None, :]).astype(jnp.int32)
    rank = lax.optimization_barrier(jnp.sum(jnp.cumsum(onehot, axis=1) * onehot, -1)) - 1
    column = jnp.arange(blocks, dtype=jnp.int32)[:, None] * MOST + rank
    table = jnp.full((EXPERTS, blocks * MOST), pair_count, jnp.int32)
    return table.at[expert_ids.reshape(-1), column.reshape(-1)].set(jnp.arange(pair_count, dtype=jnp.int32))

def full_weights(weight):
    return weight.reshape(EXPERTS, FF, D)

def pad_rows(rows):
    return jnp.concatenate([rows, jnp.zeros((1, D), rows.dtype)], 0)

def to_pairs(values, table):
    holder = jnp.zeros((TOKENS * 2 + 1, D), values.dtype)
    holder = holder.at[table.reshape(-1)].set(values.reshape(-1, D))
    return holder[:TOKENS * 2].reshape(TOKENS, 2, D)

def run_experts(rows_pad, table, gate_full, up_full, down_full):

    def one_expert(operands):
        index, gate_e, up_e, down_e = operands
        block_rows = rows_pad[index]
        gate_val = jnp.dot(block_rows, gate_e.T, preferred_element_type=jnp.float32)
        up_val = jnp.dot(block_rows, up_e.T, preferred_element_type=jnp.float32)
        hidden = (jax.nn.silu(gate_val) * up_val).astype(jnp.bfloat16)
        output = jnp.dot(hidden, down_e, preferred_element_type=jnp.float32).astype(jnp.bfloat16)
        return (output, gate_val, up_val)
    return lax.map(one_expert, (table, gate_full, up_full, down_full))

def back_experts(grad_pad, table, gate_vals, up_vals, gate_full, up_full, down_full):

    def one_expert(operands):
        index, gate_val, up_val, gate_e, up_e, down_e = operands
        grad_rows = grad_pad[index]
        grad_hidden = jnp.dot(grad_rows, down_e.T, preferred_element_type=jnp.float32)
        sigma = jax.nn.sigmoid(gate_val)
        grad_gate = (grad_hidden * up_val * sigma * (1.0 + gate_val * (1.0 - sigma))).astype(jnp.bfloat16)
        grad_up = (grad_hidden * gate_val * sigma).astype(jnp.bfloat16)
        total = jnp.dot(grad_gate, gate_e, preferred_element_type=jnp.float32)
        total = total + jnp.dot(grad_up, up_e, preferred_element_type=jnp.float32)
        return total.astype(jnp.bfloat16)
    return lax.map(one_expert, (table, gate_vals, up_vals, gate_full, up_full, down_full))

def reference(act_in, stash_in, grad_in, route_a, route_b, norm_gain, router, gate_weight, up_weight, down_weight):
    outputs = []
    input_grads = []
    router_grads = []
    gain_grads = []
    blocks = N_EXPERT * N_DP
    for segment_idx in range(N_SEGMENT):
        gain = norm_gain[segment_idx]
        router_w = router[segment_idx]
        gate_full = full_weights(gate_weight[segment_idx])
        up_full = full_weights(up_weight[segment_idx])
        down_full = full_weights(down_weight[segment_idx])
        x_float, inv_rms, normed, chosen_mask, weight_one, weight_two = prepare(act_in[segment_idx], route_a[segment_idx], gain, router_w)
        table = expert_table(route_a[segment_idx])
        expert_out, gate_vals, up_vals = run_experts(pad_rows(jnp.repeat(normed, 2, axis=0)), table, gate_full, up_full, down_full)
        pair_out = to_pairs(expert_out, table).astype(jnp.float32)
        mixed = x_float + weight_one[:, None] * pair_out[:, 0] + weight_two[:, None] * pair_out[:, 1]
        outputs.append(mixed.astype(jnp.bfloat16))
        x_float, inv_rms, normed, chosen_mask, weight_one, weight_two = prepare(stash_in[segment_idx], route_b[segment_idx], gain, router_w)
        table = expert_table(route_b[segment_idx])
        expert_out, gate_vals, up_vals = run_experts(pad_rows(jnp.repeat(normed, 2, axis=0)), table, gate_full, up_full, down_full)
        pair_out = to_pairs(expert_out, table).astype(jnp.float32)
        out_grad = grad_in[segment_idx].astype(jnp.float32)
        dot_one = lax.optimization_barrier(jnp.sum(out_grad * pair_out[:, 0], -1))
        dot_two = lax.optimization_barrier(jnp.sum(out_grad * pair_out[:, 1], -1))
        logit_grad = weight_one * weight_two * (dot_one - dot_two)
        signs = chosen_mask[:, 0].astype(jnp.float32) - chosen_mask[:, 1].astype(jnp.float32)
        dlogits = (logit_grad[:, None] * signs).astype(jnp.bfloat16)
        pair_grad = jnp.stack([weight_one[:, None] * out_grad, weight_two[:, None] * out_grad], 1).astype(jnp.bfloat16)
        grad_rows = back_experts(pad_rows(pair_grad.reshape(TOKENS * 2, D)), table, gate_vals, up_vals, gate_full, up_full, down_full)
        pair_back = to_pairs(grad_rows, table).astype(jnp.float32)
        dnormed = pair_back[:, 0] + pair_back[:, 1] + jnp.dot(dlogits, router_w, preferred_element_type=jnp.float32)
        router_grads.append(jnp.dot(dlogits.T, normed, preferred_element_type=jnp.float32) / blocks)
        gain_grads.append(lax.optimization_barrier(jnp.sum(dnormed * x_float * inv_rms, 0)) / blocks)
        dxn = dnormed * gain[None, :]
        input_grad = out_grad + inv_rms * dxn - x_float * inv_rms ** 3 * lax.optimization_barrier(jnp.mean(dxn * x_float, -1, keepdims=True))
        input_grads.append(input_grad.astype(jnp.bfloat16))
    next_act = jnp.roll(jnp.stack(outputs), 1, axis=0)
    prev_grad = jnp.roll(jnp.stack(input_grads), -1, axis=0)
    return (next_act, prev_grad, jnp.stack(router_grads), jnp.stack(gain_grads))
```

```python
import jax
import jax.numpy as jnp
from jax import lax
from jax.experimental import pallas as pl
from jax.experimental.pallas import tpu as pltpu
from jax.sharding import PartitionSpec as P

EPS = 1e-06
MOST = 8
ROWS_Z = 16
PAIRS = 8
MESH = pl.DeviceIdType.MESH
F32 = jnp.float32
BF16 = jnp.bfloat16


class Place:
    def __init__(self):
        self.seg = lax.axis_index("segment")
        self.exp = lax.axis_index("expert")
        self.dp = lax.axis_index("dp")
        self.y = self.exp // ROWS_Z
        self.z = self.exp % ROWS_Z
        self.zp = self.z // 2
        self.par = self.z % 2
        self.ny = lax.axis_size("expert") // ROWS_Z

    def owner(self, j):
        rel = j % PAIRS
        y = (self.y + j // PAIRS) % self.ny
        zp = (self.zp + rel) % PAIRS
        turn = (rel - self.par + PAIRS) % PAIRS
        exp = y * ROWS_Z + zp * 2 + turn // 4
        return (self.seg, exp, self.dp), y * PAIRS + zp, self.y * PAIRS + self.par * 4 + turn % 4

    def client(self, j):
        r = (7 * self.par + j % PAIRS) % PAIRS
        y = (self.y + j // PAIRS) % self.ny
        par = r // 4
        zp = (self.zp + 2 * PAIRS - (4 * self.par + r % 4 + par)) % PAIRS
        return (self.seg, y * ROWS_Z + zp * 2 + par, self.dp), y * PAIRS + r

    def expert(self):
        return self.y * PAIRS + self.zp

    def core(self):
        return (self.seg, self.exp, 1 - self.dp)

    def twin(self):
        return (self.seg, self.exp + 1 - 2 * self.par, self.dp)


def signal(sem, device):
    pl.semaphore_signal(sem, inc=1, device_id=device, device_id_type=MESH)


def remote(src, dst, send, recv, device):
    return pltpu.make_async_remote_copy(
        src_ref=src, dst_ref=dst, send_sem=send, recv_sem=recv, device_id=device, device_id_type=MESH
    )


def out_kernel(
    send_a, send_b, send_g, wg, wu, wd, rows, grads, gate, up, down,
    send_sem, recv_sem, own_sem, wsend, wrecv, wown,
):
    me = Place()
    count = send_a.shape[0]
    barrier = pltpu.get_barrier_semaphore()

    @pl.loop(1, count)
    def _(j):
        signal(barrier, me.client(j)[0])

    signal(barrier, me.core())
    signal(barrier, me.twin())
    pl.semaphore_wait(barrier, count + 1)

    quarter = wg.shape[0]
    weights = ((wg, gate), (wu, up), (wd, down))

    def part(ref, k):
        return ref.at[pl.ds(k * quarter, quarter)]

    for m, (own, full) in enumerate(weights):
        remote(own, part(full, 2), wsend.at[0, m], wrecv.at[0, m], me.twin()).start()
        remote(own, part(full, 1), wsend.at[1, m], wrecv.at[1, m], me.core()).start()
        pltpu.make_async_copy(own, part(full, 0), wown.at[m]).start()
    streams = ((send_a, rows.at[0]), (send_b, rows.at[1]), (send_g, grads))

    for k, (src, dst) in enumerate(streams):
        _, expert, slot = me.owner(0)
        pltpu.make_async_copy(src.at[expert], dst.at[slot], own_sem.at[k]).start()

        @pl.loop(1, count)
        def _(j):
            device, expert, slot = me.owner(j)
            remote(src.at[expert], dst.at[slot], send_sem.at[k], recv_sem.at[k], device).start()

    for m, (own, full) in enumerate(weights):
        remote(own, part(full, 2), wsend.at[0, m], wrecv.at[0, m], me.twin()).wait_recv()
        remote(part(full, 2), part(full, 3), wsend.at[2, m], wrecv.at[2, m], me.core()).start()
    for k, (src, dst) in enumerate(streams):
        whole = remote(
            src.at[pl.ds(0, count - 1)], dst.at[pl.ds(0, count - 1)], send_sem.at[k], recv_sem.at[k], me.core()
        )
        whole.wait_recv()
        whole.wait_send()
        pltpu.make_async_copy(src.at[0], dst.at[0], own_sem.at[k]).wait()
    for m, (own, full) in enumerate(weights):
        remote(own, part(full, 2), wsend.at[0, m], wrecv.at[0, m], me.twin()).wait_send()
        remote(own, part(full, 1), wsend.at[1, m], wrecv.at[1, m], me.core()).wait()
        remote(part(full, 2), part(full, 3), wsend.at[2, m], wrecv.at[2, m], me.core()).wait()
        pltpu.make_async_copy(own, part(full, 0), wown.at[m]).wait()


def back_kernel(out_a, out_b, dots, back, dots_back, send_sem, recv_sem, own_sem):
    me = Place()
    count = out_a.shape[0]
    barrier = pltpu.get_barrier_semaphore()

    @pl.loop(1, count)
    def _(j):
        signal(barrier, me.owner(j)[0])

    pl.semaphore_wait(barrier, count - 1)
    streams = ((dots, dots_back), (out_a, back.at[0]), (out_b, back.at[1]))
    expert = me.expert()
    for k, (src, dst) in enumerate(streams):
        _, slot = me.client(0)
        pltpu.make_async_copy(src.at[slot], dst.at[expert], own_sem.at[k]).start()

        @pl.loop(1, count)
        def _(j):
            device, slot = me.client(j)
            remote(src.at[slot], dst.at[expert], send_sem.at[k], recv_sem.at[k], device).start()

    for k, (src, dst) in enumerate(streams):
        whole = remote(
            src.at[pl.ds(0, count - 1)], dst.at[pl.ds(0, count - 1)], send_sem.at[k], recv_sem.at[k], me.core()
        )
        whole.wait_recv()
        whole.wait_send()
        pltpu.make_async_copy(src.at[0], dst.at[0], own_sem.at[k]).wait()


def sum_kernel(
    part, act, grad, total, next_act, prev_grad, held, got, line,
    shift_send, shift_recv, ssem, rsem,
):
    me = Place()
    ny = me.ny
    group = 2 * ny
    mine = me.y * 2 + me.dp
    barrier = pltpu.get_barrier_semaphore()
    after = ((me.seg + 1) % 4, me.exp, me.dp)
    before = ((me.seg + 3) % 4, me.exp, me.dp)

    def in_row(o):
        other = (mine + o) % group
        return other, (me.seg, (other // 2) * ROWS_Z + me.z, other % 2)

    def in_column(o):
        other = (me.z + o) % ROWS_Z
        return other, (me.seg, me.y * ROWS_Z + other, me.dp)

    signal(barrier, after)
    signal(barrier, before)

    @pl.loop(1, group)
    def _(o):
        signal(barrier, in_row(o)[1])

    @pl.loop(1, ROWS_Z)
    def _(o):
        signal(barrier, in_column(o)[1])

    pl.semaphore_wait(barrier, 2 + group - 1 + ROWS_Z - 1)
    go_next = remote(act, next_act, shift_send.at[0], shift_recv.at[0], after)
    go_prev = remote(grad, prev_grad, shift_send.at[1], shift_recv.at[1], before)

    @pl.loop(1, group)
    def _(o):
        other, device = in_row(o)
        remote(part.at[other], got.at[o - 1], ssem.at[0], rsem.at[0], device).start()

    go_next.start()
    go_prev.start()
    whole = remote(part.at[pl.ds(0, group - 1)], got, ssem.at[0], rsem.at[0], after)
    whole.wait_recv()
    held[...] = part[mine] + jnp.sum(got[...], 0)

    @pl.loop(1, ROWS_Z)
    def _(o):
        other, device = in_column(o)
        remote(held.at[other], line.at[o - 1], ssem.at[1], rsem.at[1], device).start()

    second = remote(held.at[pl.ds(0, ROWS_Z - 1)], line, ssem.at[1], rsem.at[1], after)
    second.wait_recv()
    total[mine, me.z] = held[me.z] + jnp.sum(line[...], 0)

    @pl.loop(1, ROWS_Z)
    def _(o):
        _, device = in_column(o)
        here = total.at[mine, me.z]
        remote(here, here, ssem.at[2], rsem.at[2], device).start()

    third = remote(
        total.at[mine, pl.ds(0, ROWS_Z - 1)], total.at[mine, pl.ds(0, ROWS_Z - 1)], ssem.at[2], rsem.at[2], after
    )
    third.wait_recv()

    @pl.loop(1, group)
    def _(o):
        _, device = in_row(o)
        remote(total.at[mine], total.at[mine], ssem.at[3], rsem.at[3], device).start()

    fourth = remote(
        total.at[pl.ds(0, group - 1)], total.at[pl.ds(0, group - 1)], ssem.at[3], rsem.at[3], after
    )
    fourth.wait_recv()
    whole.wait_send()
    second.wait_send()
    third.wait_send()
    fourth.wait_send()
    go_next.wait()
    go_prev.wait()


ANY = pl.BlockSpec(memory_space=pl.ANY)
VMEM = pl.BlockSpec(memory_space=pltpu.VMEM)


def params(number):
    return pltpu.CompilerParams(collective_id=number, has_side_effects=True, vmem_limit_bytes=32 << 20)


def like(shape, dtype):
    return jax.ShapeDtypeStruct(shape, dtype)


def prepare(x_block, route, gain, router_w):
    tokens = x_block.shape[0]
    experts = router_w.shape[0]
    x_float = x_block.astype(F32)
    inv_rms = lax.rsqrt(jnp.mean(x_float * x_float, -1, keepdims=True) + EPS)
    normed = (x_float * inv_rms * gain[None, :]).astype(BF16)
    logits = jnp.einsum("td,ed->te", normed, router_w, preferred_element_type=F32)
    ids = jnp.arange(experts, dtype=jnp.int32)[None, :]
    hot = (route[:, 0:1] == ids, route[:, 1:2] == ids)
    chosen = [jnp.sum(jnp.where(h, logits, 0.0), -1, keepdims=True) for h in hot]
    weights = (jax.nn.sigmoid(chosen[0] - chosen[1]), jax.nn.sigmoid(chosen[1] - chosen[0]))
    below = jnp.arange(tokens)[:, None] > jnp.arange(tokens)[None, :]
    counts = jnp.dot(below.astype(BF16), (hot[0] | hot[1]).astype(BF16), preferred_element_type=F32)
    slots = jnp.arange(experts * MOST, dtype=jnp.int32)[None, :]
    picks = []
    for k in range(2):
        rank = jnp.sum(jnp.where(hot[k], counts, 0.0), -1, keepdims=True).astype(jnp.int32)
        picks.append(route[:, k : k + 1] * MOST + rank == slots)
    return x_float, inv_rms, normed, hot, weights, picks


def to_slots(picks, rows):
    both = (picks[0] | picks[1]).astype(BF16)
    out = lax.dot_general(both, rows, (((0,), (0,)), ((), ())), preferred_element_type=F32)
    return out.astype(BF16).reshape(-1, MOST, rows.shape[1])


def from_slots(pick, slots):
    return jnp.dot(pick.astype(BF16), slots, preferred_element_type=F32)


def dot_t(a, b):
    return lax.dot_general(a, b, (((1,), (1,)), ((), ())), preferred_element_type=F32)


def body(
    act_in, stash_in, grad_in, route_a, route_b, norm_gain, router, gate_weight, up_weight, down_weight
):
    gain = norm_gain[0]
    router_w = router[0]
    experts, width = router_w.shape
    blocks = lax.axis_size("expert") * lax.axis_size("dp")
    grad = grad_in[0]
    x_a, _, normed_a, _, weights_a, picks_a = prepare(act_in[0], route_a[0], gain, router_w)
    x_b, inv_b, normed_b, hot_b, weights_b, picks_b = prepare(stash_in[0], route_b[0], gain, router_w)
    send_a = to_slots(picks_a, normed_a)
    send_b = to_slots(picks_b, normed_b)
    send_g = to_slots(picks_b, grad)
    quarters = (gate_weight[0, 0], up_weight[0, 0], down_weight[0, 0])
    quarter = quarters[0].shape[0]
    block = (experts, MOST, width)
    dma = pltpu.SemaphoreType.DMA
    rows, grads, gate, up, down = pl.pallas_call(
        out_kernel,
        out_shape=[like((2, *block), BF16), like(block, BF16)] + [like((4 * quarter, width), BF16)] * 3,
        in_specs=[ANY] * 6,
        out_specs=[ANY] * 5,
        scratch_shapes=[dma((3,)), dma((3,)), dma((3,)), dma((3, 3)), dma((3, 3)), dma((3,))],
        compiler_params=params(0),
    )(send_a, send_b, send_g, *quarters)

    slots = experts * MOST
    rows = rows.reshape(2 * slots, width)
    gate_val = dot_t(rows, gate)
    up_val = dot_t(rows, up)
    hidden = (jax.nn.silu(gate_val) * up_val).astype(BF16)
    out_a = jnp.dot(hidden[:slots], down, preferred_element_type=F32).astype(BF16).reshape(block)
    grad_hidden = dot_t(grads.reshape(slots, width), down)
    dots = jnp.sum(hidden[slots:].astype(F32) * grad_hidden, -1)
    dots = jnp.pad(dots.reshape(experts, 1, MOST), ((0, 0), (0, 0), (0, 128 - MOST)))
    gate_b, up_b = gate_val[slots:], up_val[slots:]
    sigma = jax.nn.sigmoid(gate_b)
    grad_gate = (grad_hidden * up_b * sigma * (1.0 + gate_b * (1.0 - sigma))).astype(BF16)
    grad_up = (grad_hidden * gate_b * sigma).astype(BF16)
    out_b = jnp.dot(grad_gate, gate, preferred_element_type=F32)
    out_b = out_b + jnp.dot(grad_up, up, preferred_element_type=F32)
    out_b = out_b.astype(BF16).reshape(block)

    back, dots_back = pl.pallas_call(
        back_kernel,
        out_shape=[like((2, *block), BF16), like((experts, 1, 128), F32)],
        in_specs=[ANY] * 3,
        out_specs=[ANY] * 2,
        scratch_shapes=[dma((3,)), dma((3,)), dma((3,))],
        compiler_params=params(1),
    )(out_a, out_b, dots)

    back = back.reshape(2, slots, width)
    mixed = x_a + weights_a[0] * from_slots(picks_a[0], back[0]) + weights_a[1] * from_slots(picks_a[1], back[0])
    dots_back = dots_back[:, 0, :MOST].reshape(1, slots)
    dot_of = [jnp.sum(jnp.where(pick, dots_back, 0.0), -1, keepdims=True) for pick in picks_b]
    logit_grad = weights_b[0] * weights_b[1] * (dot_of[0] - dot_of[1])
    dlogits = (logit_grad * (hot_b[0].astype(F32) - hot_b[1].astype(F32))).astype(BF16)
    out_grad = grad.astype(F32)
    dnormed = (
        weights_b[0] * from_slots(picks_b[0], back[1])
        + weights_b[1] * from_slots(picks_b[1], back[1])
        + jnp.dot(dlogits, router_w, preferred_element_type=F32)
    )
    router_term = lax.dot_general(dlogits, normed_b, (((0,), (0,)), ((), ())), preferred_element_type=F32)
    gain_term = jnp.sum(dnormed * x_b * inv_b, 0)
    dxn = dnormed * gain[None, :]
    input_grad = out_grad + inv_b * dxn - x_b * inv_b**3 * jnp.mean(dxn * x_b, -1, keepdims=True)
    group = blocks // ROWS_Z
    wide = width // ROWS_Z
    term = jnp.concatenate(
        [
            router_term.reshape(group, experts // group, ROWS_Z, wide).transpose(0, 2, 1, 3),
            jnp.pad(gain_term.reshape(1, ROWS_Z, 1, wide), ((0, group - 1), (0, 0), (0, 0), (0, 0))),
            jnp.zeros((group, ROWS_Z, 8 - experts // group - 1, wide), F32),
        ],
        2,
    )
    total, next_act, prev_grad = pl.pallas_call(
        sum_kernel,
        out_shape=[like(term.shape, F32), like(grad.shape, BF16), like(grad.shape, BF16)],
        in_specs=[VMEM, ANY, ANY],
        out_specs=[VMEM, ANY, ANY],
        scratch_shapes=[
            pltpu.VMEM(term.shape[1:], F32),
            pltpu.VMEM((group - 1, *term.shape[1:]), F32),
            pltpu.VMEM((ROWS_Z - 1, *term.shape[2:]), F32),
            dma((2,)), dma((2,)), dma((4,)), dma((4,)),
        ],
        compiler_params=params(2),
    )(term, mixed.astype(BF16), input_grad.astype(BF16))
    total = total / blocks
    router_grad = total[:, :, : experts // group].transpose(0, 2, 1, 3).reshape(experts, width)
    gain_grad = total[0, :, experts // group].reshape(width)
    return next_act[None], prev_grad[None], router_grad[None], gain_grad[None]


def solution(mesh):
    tokens = P("segment", ("expert", "dp"), None)
    weight = P("segment", "expert", "dp", None)
    router = P("segment", None, None)
    gain = P("segment", None)
    return jax.shard_map(
        body,
        mesh=mesh,
        in_specs=(tokens, tokens, tokens, tokens, tokens, gain, router, weight, weight, weight),
        out_specs=(tokens, tokens, router, gain),
        check_vma=False,
    )
```

```python
import jax
import jax.numpy as jnp
from jax import lax
from jax.experimental import pallas as pl
from jax.experimental.pallas import tpu as pltpu
from jax.sharding import PartitionSpec as P

EPS = 1e-06
MOST = 8
ROWS_Z = 16
PAIRS = 8
MESH = pl.DeviceIdType.MESH
F32 = jnp.float32
BF16 = jnp.bfloat16


class Place:
    def __init__(self):
        self.seg = lax.axis_index("segment")
        self.exp = lax.axis_index("expert")
        self.dp = lax.axis_index("dp")
        self.y = self.exp // ROWS_Z
        self.z = self.exp % ROWS_Z
        self.zp = self.z // 2
        self.par = self.z % 2
        self.ny = lax.axis_size("expert") // ROWS_Z

    def owner(self, j):
        rel = j % PAIRS
        y = (self.y + j // PAIRS) % self.ny
        zp = (self.zp + rel) % PAIRS
        turn = (rel - self.par + PAIRS) % PAIRS
        exp = y * ROWS_Z + zp * 2 + turn // 4
        return (self.seg, exp, self.dp), y * PAIRS + zp, self.y * PAIRS + self.par * 4 + turn % 4

    def client(self, j):
        r = (7 * self.par + j % PAIRS) % PAIRS
        y = (self.y + j // PAIRS) % self.ny
        par = r // 4
        zp = (self.zp + 2 * PAIRS - (4 * self.par + r % 4 + par)) % PAIRS
        return (self.seg, y * ROWS_Z + zp * 2 + par, self.dp), y * PAIRS + r

    def expert(self):
        return self.y * PAIRS + self.zp

    def core(self):
        return (self.seg, self.exp, 1 - self.dp)

    def twin(self):
        return (self.seg, self.exp + 1 - 2 * self.par, self.dp)


def signal(sem, device):
    pl.semaphore_signal(sem, inc=1, device_id=device, device_id_type=MESH)


def remote(src, dst, send, recv, device):
    return pltpu.make_async_remote_copy(
        src_ref=src, dst_ref=dst, send_sem=send, recv_sem=recv, device_id=device, device_id_type=MESH
    )


def dot(a, b, dims=((1,), (0,))):
    return lax.dot_general(a, b, (dims, ((), ())), preferred_element_type=F32)


def dot_t(a, b):
    return dot(a, b, ((1,), (1,)))


def iota(shape, axis):
    return lax.broadcasted_iota(jnp.int32, shape, axis)


def ones(mask):
    return jnp.where(mask, 1.0, 0.0)


def norm_of(x):
    x_float = x.astype(F32)
    inv_rms = lax.rsqrt(jnp.mean(x_float * x_float, -1, keepdims=True) + EPS)
    return x_float, inv_rms


def prepare(x, route, gain, router_w):
    tokens = x.shape[0]
    experts = router_w.shape[0]
    x_float, inv_rms = norm_of(x)
    normed = (x_float * inv_rms * gain).astype(BF16)
    logits = dot_t(normed, router_w)
    ids = iota((tokens, experts), 1)
    hot = [ones(route[:, k : k + 1] == ids) for k in range(2)]
    chosen = [jnp.sum(h * logits, -1, keepdims=True) for h in hot]
    weights = (jax.nn.sigmoid(chosen[0] - chosen[1]), jax.nn.sigmoid(chosen[1] - chosen[0]))
    below = ones(iota((tokens, tokens), 0) > iota((tokens, tokens), 1)).astype(BF16)
    counts = dot(below, (hot[0] + hot[1]).astype(BF16))
    slots = iota((tokens, experts * MOST), 1)
    picks = []
    for k in range(2):
        rank = jnp.sum(hot[k] * counts, -1, keepdims=True).astype(jnp.int32)
        picks.append(ones(route[:, k : k + 1] * MOST + rank == slots))
    return normed, weights, picks


def to_slots(both, rows):
    out = dot(both, rows, ((0,), (0,)))
    return out.reshape(out.shape[0] // MOST, MOST, out.shape[1]).astype(BF16)


def flat(blocks):
    return blocks.astype(F32).reshape(blocks.shape[0] * MOST, blocks.shape[2]).astype(BF16)


def kernel(
    act, stash, grad, route_a, route_b, gain, router, wg, wu, wd,
    next_act, prev_grad, router_out, gain_out,
    send_a, send_b, send_g, rec_a, rec_b, rec_g, rows, grads, gate, up, down, acc,
    out_a, out_b, back_a, back_b, normed_b, mixed,
    stash_s, grad_s, picks_b, picks_s, router_s, gain_s, dlog, dlog_s,
    p_send, p_rec, q_send, q_back, rsum, term, held, got, line, total,
    ssem, rsem, own, shift_send, shift_recv, wsend, wrecv, wown, sum_send, sum_recv,
):
    me = Place()
    count = send_a.shape[0]
    tokens = act.shape[0]
    quarters = gate.shape[0]
    width = act.shape[1]
    group = 2 * me.ny
    mine = me.y * 2 + me.dp
    behind, ahead = (me.seg + 3) % 4, (me.seg + 1) % 4
    before = (behind, me.exp, me.dp)
    after = (ahead, me.exp, me.dp)
    barrier = pltpu.get_barrier_semaphore()

    def in_row(o):
        other = (mine + o) % group
        return other, (me.seg, (other // 2) * ROWS_Z + me.z, other % 2)

    def in_column(o):
        other = (me.z + o) % ROWS_Z
        return other, (me.seg, me.y * ROWS_Z + other, me.dp)

    signal(barrier, before)
    signal(barrier, me.core())
    signal(barrier, me.twin())
    signal(barrier, after)

    @pl.loop(1, count)
    def _(j):
        signal(barrier, me.client(j)[0])
        device = me.owner(j)[0]
        signal(barrier, device)
        signal(barrier, (ahead, device[1], device[2]))

    @pl.loop(1, group)
    def _(o):
        signal(barrier, in_row(o)[1])

    @pl.loop(1, ROWS_Z)
    def _(o):
        signal(barrier, in_column(o)[1])

    pl.semaphore_wait(barrier, 4 + 3 * (count - 1) + group - 1 + ROWS_Z - 1)

    weights = ((wg, gate), (wu, up), (wd, down))

    def to_twin(m):
        return remote(weights[m][0], weights[m][1].at[2], wsend.at[0, m], wrecv.at[0, m], me.twin())

    def to_core(m):
        return remote(weights[m][0], weights[m][1].at[1], wsend.at[1, m], wrecv.at[1, m], me.core())

    def on_to_core(m):
        full = weights[m][1]
        return remote(full.at[2], full.at[3], wsend.at[2, m], wrecv.at[2, m], me.core())

    def to_self(m):
        return pltpu.make_async_copy(weights[m][0], weights[m][1].at[0], wown.at[m])

    def shift(k, src, dst, device):
        return remote(src, dst, shift_send.at[k], shift_recv.at[k], device)

    shifts = [
        shift(0, stash, stash_s, before),
        shift(1, grad, grad_s, before),
        shift(2, router, router_s, before),
        shift(3, gain, gain_s, before),
        shift(4, picks_b, picks_s, before),
        shift(5, dlog, dlog_s, before),
        shift(6, mixed, next_act, after),
    ]

    def send(k, src, dst, block=lambda e: e):
        _, expert, slot = me.owner(0)
        pltpu.make_async_copy(src.at[block(expert)], dst.at[slot], own.at[k]).start()

        @pl.loop(1, count)
        def _(j):
            device, expert, slot = me.owner(j)
            remote(src.at[block(expert)], dst.at[slot], ssem.at[k], rsem.at[k], device).start()

    def send_back(k, src, dst):
        expert = me.expert()
        pltpu.make_async_copy(src.at[me.client(0)[1]], dst.at[expert], own.at[k]).start()

        @pl.loop(1, count)
        def _(j):
            device, slot = me.client(j)
            remote(src.at[slot], dst.at[expert], ssem.at[k], rsem.at[k], device).start()

    def others(k, ref):
        part = ref.at[pl.ds(0, count - 1)]
        return remote(part, part, ssem.at[k], rsem.at[k], after)

    def arrived(k, ref):
        others(k, ref).wait_recv()
        pltpu.make_async_copy(ref.at[0], ref.at[0], own.at[k]).wait()

    for m in range(3):
        to_twin(m).start()
        to_core(m).start()
        to_self(m).start()
    gain_row = gain[...]
    normed_a, weights_a, picks_a = prepare(act[...], route_a[...], gain_row, router[...])
    send_a[...] = to_slots((picks_a[0] + picks_a[1]).astype(BF16), normed_a)
    send(0, send_a, rec_a)
    for k in range(4):
        shifts[k].start()

    normed, weights_b, picks = prepare(stash[...], route_b[...], gain_row, router[...])
    normed_b[...] = normed
    both = (picks[0] + picks[1]).astype(BF16)
    picks_b[...] = both
    shifts[4].start()
    send_b[...] = to_slots(both, normed)
    send(1, send_b, rec_b)
    send_g[...] = to_slots(both, grad[...])
    send(2, send_g, rec_g)
    p_row = jnp.sum(picks[0] * weights_b[0] + picks[1] * weights_b[1], 0, keepdims=True)
    halves = p_send.shape[0]
    for h in range(halves):
        p_send[h] = p_row[:, h * 128 : (h + 1) * 128]
    per_half = count // halves
    send(3, p_send, p_rec, lambda e: e // per_half)

    for m in range(3):
        to_twin(m).wait_recv()
        on_to_core(m).start()
    arrived(0, rec_a)
    rows[...] = flat(rec_a[...])
    for m in range(3):
        to_core(m).wait_recv()
        on_to_core(m).wait_recv()
        to_self(m).wait()
    acc[...] = jnp.zeros_like(acc)

    @pl.loop(0, quarters)
    def _(c):
        gate_val = dot_t(rows[...], gate[c])
        up_val = dot_t(rows[...], up[c])
        hidden = (gate_val * jax.nn.sigmoid(gate_val) * up_val).astype(BF16)
        acc[...] += dot(hidden, down[c])

    out_a[...] = acc[...].reshape(out_a.shape).astype(BF16)
    arrived(1, rec_b)
    arrived(2, rec_g)
    arrived(3, p_rec)
    send_back(4, out_a, back_a)

    rows[...] = flat(rec_b[...])
    grads[...] = flat(rec_g[...])
    acc[...] = jnp.zeros_like(acc)
    slots = count * MOST

    def back_part(c, dots):
        gate_val = dot_t(rows[...], gate[c])
        up_val = dot_t(rows[...], up[c])
        grad_hidden = dot_t(grads[...], down[c])
        sigma = jax.nn.sigmoid(gate_val)
        silu = gate_val * sigma
        hidden = (silu * up_val).astype(BF16)
        grad_gate = (grad_hidden * up_val * sigma * (1.0 + gate_val * (1.0 - sigma))).astype(BF16)
        grad_up = (grad_hidden * silu).astype(BF16)
        acc[...] += dot(grad_gate, gate[c]) + dot(grad_up, up[c])
        return dots + jnp.sum(hidden.astype(F32) * grad_hidden, -1, keepdims=True)

    dots = lax.fori_loop(0, quarters, back_part, jnp.zeros((slots, 1), F32))
    base = (me.expert() % per_half) * MOST
    lanes = ones(iota((count, MOST, 128), 2) == iota((count, MOST, 128), 1) + base)
    q_send[...] = jnp.sum(lanes * dots.reshape(count, MOST, 1), 1, keepdims=True)
    send_back(5, q_send, q_back)
    p_col = jnp.sum(lanes * p_rec[...], 2, keepdims=True).reshape(slots, 1)
    scaled = acc[...] * p_col
    out_b[...] = scaled.reshape(out_b.shape).astype(BF16)
    expert = me.expert()

    @pl.loop(0, count)
    def _(j):
        device, slot = me.client(j)
        device = (behind, device[1], device[2])
        remote(out_b.at[slot], back_b.at[expert], ssem.at[6], rsem.at[6], device).start()

    gain_own = jnp.sum(scaled * rows[...].astype(F32), 0, keepdims=True) / gain_row

    arrived(5, q_back)
    q_all = q_back[...]
    q_row = jnp.concatenate(
        [jnp.sum(q_all[h * per_half : (h + 1) * per_half], 0) for h in range(halves)], 1
    )
    dot_of = [jnp.sum(pick * q_row, -1, keepdims=True) for pick in picks]
    logit_grad = weights_b[0] * weights_b[1] * (dot_of[0] - dot_of[1])
    ids = iota((tokens, 128), 1)
    route = route_b[...]
    signs = ones(route[:, 0:1] == ids) - ones(route[:, 1:2] == ids)
    dlogits = (logit_grad * signs).astype(BF16)
    dlog[...] = dlogits
    shifts[5].start()
    x_float, inv_rms = norm_of(stash[...])
    dlogits = dlogits[:, :count]
    rsum[...] = dot(dlogits, normed_b[...], ((0,), (0,)))
    gain_part = gain_own + jnp.sum(dot(dlogits, router[...]) * x_float * inv_rms, 0, keepdims=True)
    per = count // group
    term[...] = jnp.zeros_like(term)
    for g in range(group):
        for c in range(ROWS_Z):
            term[g, c, 0:per, :] = rsum[g * per : (g + 1) * per, c * 128 : (c + 1) * 128]
    for c in range(ROWS_Z):
        term[0, c, per : per + 1, :] = gain_part[:, c * 128 : (c + 1) * 128]

    @pl.loop(1, group)
    def _(o):
        other, device = in_row(o)
        remote(term.at[other], got.at[o - 1], sum_send.at[0], sum_recv.at[0], device).start()

    def summed(k, ref):
        return remote(ref, ref, sum_send.at[k], sum_recv.at[k], after)

    summed(0, got).wait_recv()
    held[...] = term[mine] + jnp.sum(got[...], 0)

    @pl.loop(1, ROWS_Z)
    def _(o):
        other, device = in_column(o)
        remote(held.at[other], line.at[o - 1], sum_send.at[1], sum_recv.at[1], device).start()

    summed(1, line).wait_recv()
    total[mine, me.z] = held[me.z] + jnp.sum(line[...], 0)

    @pl.loop(1, ROWS_Z)
    def _(o):
        here = total.at[mine, me.z]
        remote(here, here, sum_send.at[2], sum_recv.at[2], in_column(o)[1]).start()

    summed(2, line).wait_recv()

    @pl.loop(1, group)
    def _(o):
        remote(total.at[mine], total.at[mine], sum_send.at[3], sum_recv.at[3], in_row(o)[1]).start()

    arrived(4, back_a)
    returned = flat(back_a[...])
    mixed[...] = (
        act[...].astype(F32)
        + weights_a[0] * dot(picks_a[0].astype(BF16), returned)
        + weights_a[1] * dot(picks_a[1].astype(BF16), returned)
    ).astype(BF16)
    shifts[6].start()

    summed(3, got).wait_recv()
    scale = 1.0 / (group * ROWS_Z)
    for g in range(group):
        for c in range(ROWS_Z):
            router_out[g * per : (g + 1) * per, c * 128 : (c + 1) * 128] = total[g, c, 0:per, :] * scale
    for c in range(ROWS_Z):
        gain_out[:, c * 128 : (c + 1) * 128] = total[0, c, per : per + 1, :] * scale

    for k in range(6):
        shifts[k].wait_recv()
    x_float, inv_rms = norm_of(stash_s[...])
    acc[0:tokens, :] = dot(dlog_s[...][:, :count], router_s[...])
    remote(out_b, back_b, ssem.at[6], rsem.at[6], after).wait_recv()
    dnormed = acc[0:tokens, :] + dot(picks_s[...], flat(back_b[...]))
    dxn = dnormed * gain_s[...]
    prev_grad[...] = (
        grad_s[...].astype(F32)
        + inv_rms * dxn
        - x_float * (inv_rms * inv_rms * inv_rms * jnp.mean(dxn * x_float, -1, keepdims=True))
    ).astype(BF16)

    for m in range(3):
        to_twin(m).wait_send()
        to_core(m).wait_send()
        on_to_core(m).wait_send()
    for k, ref in enumerate((rec_a, rec_b, rec_g, p_rec, back_a, q_back)):
        others(k, ref).wait_send()
    remote(out_b, back_b, ssem.at[6], rsem.at[6], after).wait_send()
    for k in range(7):
        shifts[k].wait_send()
    shifts[6].wait_recv()
    for k, ref in enumerate((got, line, line, got)):
        summed(k, ref).wait_send()


ANY = pl.BlockSpec(memory_space=pl.ANY)
VMEM = pl.BlockSpec(memory_space=pltpu.VMEM)


def like(shape, dtype):
    return jax.ShapeDtypeStruct(shape, dtype)


def body(
    act_in, stash_in, grad_in, route_a, route_b, norm_gain, router, gate_weight, up_weight, down_weight
):
    tokens, width = act_in.shape[1:]
    experts = router.shape[1]
    quarter = gate_weight.shape[2]
    group = lax.axis_size("expert") * lax.axis_size("dp") // ROWS_Z
    slots = experts * MOST
    block = (experts, MOST, width)
    dma = pltpu.SemaphoreType.DMA

    def vb(*shape):
        return pltpu.VMEM(shape, BF16)

    def vf(*shape):
        return pltpu.VMEM(shape, F32)

    full = vb(4, quarter, width)
    row = (tokens, width)
    lanes = (experts, 1, 128)
    next_act, prev_grad, router_grad, gain_grad = pl.pallas_call(
        kernel,
        out_shape=[like(row, BF16), like(row, BF16), like((experts, width), F32), like((1, width), F32)],
        in_specs=[VMEM] * 7 + [ANY] * 3,
        out_specs=[VMEM] * 4,
        scratch_shapes=[vb(*block)] * 6
        + [vb(slots, width)] * 2
        + [full] * 3
        + [vf(slots, width)]
        + [vb(*block)] * 4
        + [vb(*row)] * 2
        + [vb(*row)] * 2
        + [vb(tokens, slots)] * 2
        + [vb(experts, width), vf(1, width)]
        + [vb(tokens, 128)] * 2
        + [vf(slots // 128, 1, 128), vf(*lanes), vf(*lanes), vf(*lanes)]
        + [vf(experts, width), vf(group, ROWS_Z, 8, 128), vf(ROWS_Z, 8, 128)]
        + [vf(group - 1, ROWS_Z, 8, 128), vf(ROWS_Z - 1, 8, 128), vf(group, ROWS_Z, 8, 128)]
        + [dma((7,)), dma((7,)), dma((6,)), dma((7,)), dma((7,))]
        + [dma((3, 3)), dma((3, 3)), dma((3,)), dma((4,)), dma((4,))],
        compiler_params=pltpu.CompilerParams(
            collective_id=0, has_side_effects=True, vmem_limit_bytes=56 << 20
        ),
    )(
        act_in[0], stash_in[0], grad_in[0], route_a[0], route_b[0], norm_gain, router[0],
        gate_weight[0, 0], up_weight[0, 0], down_weight[0, 0],
    )
    return next_act[None], prev_grad[None], router_grad[None], gain_grad


def solution(mesh):
    tokens = P("segment", ("expert", "dp"), None)
    weight = P("segment", "expert", "dp", None)
    router = P("segment", None, None)
    gain = P("segment", None)
    return jax.shard_map(
        body,
        mesh=mesh,
        in_specs=(tokens, tokens, tokens, tokens, tokens, gain, router, weight, weight, weight),
        out_specs=(tokens, tokens, router, gain),
        check_vma=False,
    )
```

```python
import jax
import jax.numpy as jnp
from jax import lax
from jax.experimental import pallas as pl
from jax.experimental.pallas import tpu as pltpu
from jax.sharding import PartitionSpec as P

EPS = 1e-06
MOST = 8
ROWS_Z = 16
PAIRS = 8
MESH = pl.DeviceIdType.MESH
F32 = jnp.float32
BF16 = jnp.bfloat16


class Place:
    def __init__(self):
        self.seg = lax.axis_index("segment")
        self.exp = lax.axis_index("expert")
        self.dp = lax.axis_index("dp")
        self.y = self.exp // ROWS_Z
        self.z = self.exp % ROWS_Z
        self.zp = self.z // 2
        self.par = self.z % 2
        self.ny = lax.axis_size("expert") // ROWS_Z

    def owner(self, j):
        rel = j % PAIRS
        y = (self.y + j // PAIRS) % self.ny
        zp = (self.zp + rel) % PAIRS
        turn = (rel - self.par + PAIRS) % PAIRS
        exp = y * ROWS_Z + zp * 2 + turn // 4
        return (self.seg, exp, self.dp), y * PAIRS + zp, self.y * PAIRS + self.par * 4 + turn % 4

    def client(self, j):
        r = (7 * self.par + j % PAIRS) % PAIRS
        y = (self.y + j // PAIRS) % self.ny
        par = r // 4
        zp = (self.zp + 2 * PAIRS - (4 * self.par + r % 4 + par)) % PAIRS
        return (self.seg, y * ROWS_Z + zp * 2 + par, self.dp), y * PAIRS + r

    def expert(self):
        return self.y * PAIRS + self.zp

    def core(self):
        return (self.seg, self.exp, 1 - self.dp)

    def twin(self):
        return (self.seg, self.exp + 1 - 2 * self.par, self.dp)


def signal(sem, device):
    pl.semaphore_signal(sem, inc=1, device_id=device, device_id_type=MESH)


def remote(src, dst, send, recv, device):
    return pltpu.make_async_remote_copy(
        src_ref=src, dst_ref=dst, send_sem=send, recv_sem=recv, device_id=device, device_id_type=MESH
    )


def dot(a, b, dims=((1,), (0,))):
    return lax.dot_general(a, b, (dims, ((), ())), preferred_element_type=F32)


def dot_t(a, b):
    return dot(a, b, ((1,), (1,)))


def iota(shape, axis):
    return lax.broadcasted_iota(jnp.int32, shape, axis)


def ones(mask):
    return jnp.where(mask, 1.0, 0.0)


def norm_of(x):
    x_float = x.astype(F32)
    inv_rms = lax.rsqrt(jnp.mean(x_float * x_float, -1, keepdims=True) + EPS)
    return x_float, inv_rms


def prepare(x, route, gain, router_w):
    tokens = x.shape[0]
    experts = router_w.shape[0]
    x_float, inv_rms = norm_of(x)
    normed = (x_float * inv_rms * gain).astype(BF16)
    logits = dot_t(normed, router_w)
    ids = iota((tokens, experts), 1)
    hot = [ones(route[:, k : k + 1] == ids) for k in range(2)]
    chosen = [jnp.sum(h * logits, -1, keepdims=True) for h in hot]
    weights = (jax.nn.sigmoid(chosen[0] - chosen[1]), jax.nn.sigmoid(chosen[1] - chosen[0]))
    below = ones(iota((tokens, tokens), 0) > iota((tokens, tokens), 1)).astype(BF16)
    counts = dot(below, (hot[0] + hot[1]).astype(BF16))
    slots = iota((tokens, experts * MOST), 1)
    picks = []
    for k in range(2):
        rank = jnp.sum(hot[k] * counts, -1, keepdims=True).astype(jnp.int32)
        picks.append(ones(route[:, k : k + 1] * MOST + rank == slots))
    return normed, weights, picks


def to_slots(both, rows):
    out = dot(both, rows, ((0,), (0,)))
    return out.reshape(out.shape[0] // MOST, MOST, out.shape[1]).astype(BF16)


def flat(blocks):
    return blocks.astype(F32).reshape(blocks.shape[0] * MOST, blocks.shape[2]).astype(BF16)


def kernel(
    act, stash, grad, routes, gain, router, wg, wu, wd,
    next_act, prev_grad, router_out, gain_out,
    send_a, send_b, send_g, rec_a, rec_b, rec_g, rows, grads, gate, up, down, acc,
    out_a, out_b, back_a, back_b, normed_b, mixed,
    stash_s, grad_s, picks_b, picks_s, router_s, gain_s, dlog, dlog_s,
    p_send, p_rec, q_send, q_back, rsum, wide, term, held, got, line, total,
    ssem, rsem, own, shift_send, shift_recv, wsend, wrecv, wown, sum_send, sum_recv,
):
    me = Place()
    count = send_a.shape[0]
    tokens = act.shape[0]
    quarters = gate.shape[0]
    width = act.shape[1]
    group = 2 * me.ny
    mine = me.y * 2 + me.dp
    behind, ahead = (me.seg + 3) % 4, (me.seg + 1) % 4
    before = (behind, me.exp, me.dp)
    after = (ahead, me.exp, me.dp)
    barrier = pltpu.get_barrier_semaphore()

    def in_row(o):
        other = (mine + o) % group
        return other, (me.seg, (other // 2) * ROWS_Z + me.z, other % 2)

    def in_column(o):
        other = (me.z + o) % ROWS_Z
        return other, (me.seg, me.y * ROWS_Z + other, me.dp)

    signal(barrier, before)
    signal(barrier, me.core())
    signal(barrier, me.twin())
    signal(barrier, after)

    @pl.loop(1, count)
    def _(j):
        signal(barrier, me.client(j)[0])
        device = me.owner(j)[0]
        signal(barrier, device)
        signal(barrier, (ahead, device[1], device[2]))

    @pl.loop(1, group)
    def _(o):
        signal(barrier, in_row(o)[1])

    @pl.loop(1, ROWS_Z)
    def _(o):
        signal(barrier, in_column(o)[1])

    pl.semaphore_wait(barrier, 4 + 3 * (count - 1) + group - 1 + ROWS_Z - 1)

    weights = ((wg, gate), (wu, up), (wd, down))

    def to_twin(m):
        return remote(weights[m][0], weights[m][1].at[2], wsend.at[0, m], wrecv.at[0, m], me.twin())

    def to_core(m):
        return remote(weights[m][0], weights[m][1].at[1], wsend.at[1, m], wrecv.at[1, m], me.core())

    def on_to_core(m):
        full = weights[m][1]
        return remote(full.at[2], full.at[3], wsend.at[2, m], wrecv.at[2, m], me.core())

    def to_self(m):
        return pltpu.make_async_copy(weights[m][0], weights[m][1].at[0], wown.at[m])

    def shift(k, src, dst, device):
        return remote(src, dst, shift_send.at[k], shift_recv.at[k], device)

    shifts = [
        shift(0, stash, stash_s, before),
        shift(1, grad, grad_s, before),
        shift(2, router, router_s, before),
        shift(3, gain, gain_s, before),
        shift(4, picks_b, picks_s, before),
        shift(5, dlog, dlog_s, before),
        shift(6, mixed, next_act, after),
    ]

    def send(k, src, dst, block=lambda e: e):
        _, expert, slot = me.owner(0)
        pltpu.make_async_copy(src.at[block(expert)], dst.at[slot], own.at[k]).start()

        @pl.loop(1, count)
        def _(j):
            device, expert, slot = me.owner(j)
            remote(src.at[block(expert)], dst.at[slot], ssem.at[k], rsem.at[k], device).start()

    expert = me.expert()

    def keep_back(k, src, dst):
        pltpu.make_async_copy(src.at[me.client(0)[1]], dst.at[expert], own.at[k]).start()

    def send_back(k, src, dst, first, last):
        @pl.loop(first, last)
        def _(j):
            device, slot = me.client(j)
            remote(src.at[slot], dst.at[expert], ssem.at[k], rsem.at[k], device).start()

    def others(k, ref):
        part = ref.at[pl.ds(0, count - 1)]
        return remote(part, part, ssem.at[k], rsem.at[k], after)

    def arrived(k, ref):
        others(k, ref).wait_recv()
        pltpu.make_async_copy(ref.at[0], ref.at[0], own.at[k]).wait()

    for m in range(3):
        to_twin(m).start()
        to_core(m).start()
        to_self(m).start()
    gain_row = gain[...]
    normed_a, weights_a, picks_a = prepare(act[...], routes[:, 0:2], gain_row, router[...])
    send_a[...] = to_slots((picks_a[0] + picks_a[1]).astype(BF16), normed_a)
    send(0, send_a, rec_a)

    normed, weights_b, picks = prepare(stash[...], routes[:, 2:4], gain_row, router[...])
    normed_b[...] = normed
    both = (picks[0] + picks[1]).astype(BF16)
    picks_b[...] = both
    shifts[4].start()
    send_b[...] = to_slots(both, normed)
    send(1, send_b, rec_b)
    send_g[...] = to_slots(both, grad[...])
    send(2, send_g, rec_g)
    for k in range(4):
        shifts[k].start()
    p_row = jnp.sum(picks[0] * weights_b[0] + picks[1] * weights_b[1], 0, keepdims=True)
    halves = p_send.shape[0]
    for h in range(halves):
        p_send[h] = p_row[:, h * 128 : (h + 1) * 128]
    per_half = count // halves
    send(3, p_send, p_rec, lambda e: e // per_half)

    for m in range(3):
        to_twin(m).wait_recv()
        on_to_core(m).start()
    arrived(0, rec_a)
    rows[...] = flat(rec_a[...])
    for m in range(3):
        to_core(m).wait_recv()
        on_to_core(m).wait_recv()
        to_self(m).wait()
    acc[...] = jnp.zeros_like(acc)

    @pl.loop(0, quarters)
    def _(c):
        gate_val = dot_t(rows[...], gate[c])
        up_val = dot_t(rows[...], up[c])
        hidden = (gate_val * jax.nn.sigmoid(gate_val) * up_val).astype(BF16)
        acc[...] += dot(hidden, down[c])

    out_a[...] = acc[...].reshape(out_a.shape).astype(BF16)
    keep_back(4, out_a, back_a)
    send_back(4, out_a, back_a, 1, count // 2)
    arrived(1, rec_b)
    arrived(2, rec_g)
    arrived(3, p_rec)
    send_back(4, out_a, back_a, count // 2, count)

    rows[...] = flat(rec_b[...])
    grads[...] = flat(rec_g[...])
    acc[...] = jnp.zeros_like(acc)
    slots = count * MOST

    def back_part(c, dots):
        gate_val = dot_t(rows[...], gate[c])
        up_val = dot_t(rows[...], up[c])
        grad_hidden = dot_t(grads[...], down[c])
        sigma = jax.nn.sigmoid(gate_val)
        silu = gate_val * sigma
        hidden = (silu * up_val).astype(BF16)
        grad_gate = (grad_hidden * up_val * sigma * (1.0 + gate_val * (1.0 - sigma))).astype(BF16)
        grad_up = (grad_hidden * silu).astype(BF16)
        acc[...] += dot(grad_gate, gate[c]) + dot(grad_up, up[c])
        return dots + jnp.sum(hidden.astype(F32) * grad_hidden, -1, keepdims=True)

    dots = lax.fori_loop(0, quarters, back_part, jnp.zeros((slots, 1), F32))
    base = (me.expert() % per_half) * MOST
    lanes = ones(iota((count, MOST, 128), 2) == iota((count, MOST, 128), 1) + base)
    q_send[...] = jnp.sum(lanes * dots.reshape(count, MOST, 1), 1, keepdims=True)
    keep_back(5, q_send, q_back)
    send_back(5, q_send, q_back, 1, count)
    p_col = jnp.sum(lanes * p_rec[...], 2, keepdims=True).reshape(slots, 1)
    scaled = acc[...] * p_col
    out_b[...] = scaled.reshape(out_b.shape).astype(BF16)

    def grads_back(part):
        @pl.loop(part * count // 4, (part + 1) * count // 4)
        def _(j):
            device, slot = me.client(j)
            device = (behind, device[1], device[2])
            remote(out_b.at[slot], back_b.at[expert], ssem.at[6], rsem.at[6], device).start()

    grads_back(0)
    gain_own = jnp.sum(scaled * rows[...].astype(F32), 0, keepdims=True) / gain_row

    arrived(5, q_back)
    q_all = q_back[...]
    q_row = jnp.concatenate(
        [jnp.sum(q_all[h * per_half : (h + 1) * per_half], 0) for h in range(halves)], 1
    )
    dot_of = [jnp.sum(pick * q_row, -1, keepdims=True) for pick in picks]
    logit_grad = weights_b[0] * weights_b[1] * (dot_of[0] - dot_of[1])
    ids = iota((tokens, 128), 1)
    signs = ones(routes[:, 2:3] == ids) - ones(routes[:, 3:4] == ids)
    dlogits = (logit_grad * signs).astype(BF16)
    dlog[...] = dlogits
    shifts[5].start()
    x_float, inv_rms = norm_of(stash[...])
    dlogits = dlogits[:, :count]
    rsum[...] = dot(dlogits, normed_b[...], ((0,), (0,)))
    gain_part = gain_own + jnp.sum(dot(dlogits, router[...]) * x_float * inv_rms, 0, keepdims=True)
    per = count // group
    wide[...] = jnp.zeros_like(wide)
    for g in range(group):
        for c in range(ROWS_Z):
            wide[g, c, 0:per, :] = rsum[g * per : (g + 1) * per, c * 128 : (c + 1) * 128]
    for c in range(ROWS_Z):
        wide[0, c, per : per + 1, :] = gain_part[:, c * 128 : (c + 1) * 128]
    term[...] = wide[...].astype(BF16)

    @pl.loop(1, group)
    def _(o):
        other, device = in_row(o)
        remote(term.at[other], got.at[o - 1], sum_send.at[0], sum_recv.at[0], device).start()

    def summed(k, ref):
        return remote(ref, ref, sum_send.at[k], sum_recv.at[k], after)

    grads_back(1)
    summed(0, got).wait_recv()
    held[...] = (wide[mine] + jnp.sum(got[...].astype(F32), 0)).astype(BF16)

    @pl.loop(1, ROWS_Z)
    def _(o):
        other, device = in_column(o)
        remote(held.at[other], line.at[o - 1], sum_send.at[1], sum_recv.at[1], device).start()

    grads_back(2)
    summed(1, line).wait_recv()
    total[mine, me.z] = (held[me.z].astype(F32) + jnp.sum(line[...].astype(F32), 0)).astype(BF16)

    @pl.loop(1, ROWS_Z)
    def _(o):
        here = total.at[mine, me.z]
        remote(here, here, sum_send.at[2], sum_recv.at[2], in_column(o)[1]).start()

    grads_back(3)
    summed(2, line).wait_recv()

    @pl.loop(1, group)
    def _(o):
        remote(total.at[mine], total.at[mine], sum_send.at[3], sum_recv.at[3], in_row(o)[1]).start()

    arrived(4, back_a)
    returned = flat(back_a[...])
    mixed[...] = (
        act[...].astype(F32)
        + weights_a[0] * dot(picks_a[0].astype(BF16), returned)
        + weights_a[1] * dot(picks_a[1].astype(BF16), returned)
    ).astype(BF16)
    shifts[6].start()

    summed(3, got).wait_recv()
    scale = 1.0 / (group * ROWS_Z)
    wide[...] = total[...].astype(F32) * scale
    for g in range(group):
        for c in range(ROWS_Z):
            router_out[g * per : (g + 1) * per, c * 128 : (c + 1) * 128] = wide[g, c, 0:per, :]
    for c in range(ROWS_Z):
        gain_out[:, c * 128 : (c + 1) * 128] = wide[0, c, per : per + 1, :]

    for k in range(6):
        shifts[k].wait_recv()
    x_float, inv_rms = norm_of(stash_s[...])
    acc[0:tokens, :] = dot(dlog_s[...][:, :count], router_s[...])
    remote(out_b, back_b, ssem.at[6], rsem.at[6], after).wait_recv()
    dnormed = acc[0:tokens, :] + dot(picks_s[...], flat(back_b[...]))
    dxn = dnormed * gain_s[...]
    prev_grad[...] = (
        grad_s[...].astype(F32)
        + inv_rms * dxn
        - x_float * (inv_rms * inv_rms * inv_rms * jnp.mean(dxn * x_float, -1, keepdims=True))
    ).astype(BF16)

    for m in range(3):
        to_twin(m).wait_send()
        to_core(m).wait_send()
        on_to_core(m).wait_send()
    for k, ref in enumerate((rec_a, rec_b, rec_g, p_rec, back_a, q_back)):
        others(k, ref).wait_send()
    remote(out_b, back_b, ssem.at[6], rsem.at[6], after).wait_send()
    for k in range(7):
        shifts[k].wait_send()
    shifts[6].wait_recv()
    for k, ref in enumerate((got, line, line, got)):
        summed(k, ref).wait_send()


ANY = pl.BlockSpec(memory_space=pl.ANY)
VMEM = pl.BlockSpec(memory_space=pltpu.VMEM)


def like(shape, dtype):
    return jax.ShapeDtypeStruct(shape, dtype)


def body(
    act_in, stash_in, grad_in, route_a, route_b, norm_gain, router, gate_weight, up_weight, down_weight
):
    tokens, width = act_in.shape[1:]
    experts = router.shape[1]
    quarter = gate_weight.shape[2]
    group = lax.axis_size("expert") * lax.axis_size("dp") // ROWS_Z
    slots = experts * MOST
    block = (experts, MOST, width)
    dma = pltpu.SemaphoreType.DMA

    def vb(*shape):
        return pltpu.VMEM(shape, BF16)

    def vf(*shape):
        return pltpu.VMEM(shape, F32)

    full = vb(4, quarter, width)
    row = (tokens, width)
    lanes = (experts, 1, 128)
    next_act, prev_grad, router_grad, gain_grad = pl.pallas_call(
        kernel,
        out_shape=[like(row, BF16), like(row, BF16), like((experts, width), F32), like((1, width), F32)],
        in_specs=[VMEM] * 6 + [ANY] * 3,
        out_specs=[VMEM] * 4,
        scratch_shapes=[vb(*block)] * 6
        + [vb(slots, width)] * 2
        + [full] * 3
        + [vf(slots, width)]
        + [vb(*block)] * 4
        + [vb(*row)] * 2
        + [vb(*row)] * 2
        + [vb(tokens, slots)] * 2
        + [vb(experts, width), vf(1, width)]
        + [vb(tokens, 128)] * 2
        + [vf(slots // 128, 1, 128), vf(*lanes), vf(*lanes), vf(*lanes)]
        + [vf(experts, width), vf(group, ROWS_Z, 8, 128), vb(group, ROWS_Z, 8, 128), vb(ROWS_Z, 8, 128)]
        + [vb(group - 1, ROWS_Z, 8, 128), vb(ROWS_Z - 1, 8, 128), vb(group, ROWS_Z, 8, 128)]
        + [dma((7,)), dma((7,)), dma((6,)), dma((7,)), dma((7,))]
        + [dma((3, 3)), dma((3, 3)), dma((3,)), dma((4,)), dma((4,))],
        compiler_params=pltpu.CompilerParams(
            collective_id=0, has_side_effects=True, vmem_limit_bytes=56 << 20
        ),
    )(
        act_in[0], stash_in[0], grad_in[0], jnp.concatenate([route_a[0], route_b[0]], 1), norm_gain, router[0],
        gate_weight[0, 0], up_weight[0, 0], down_weight[0, 0],
    )
    return next_act[None], prev_grad[None], router_grad[None], gain_grad


def solution(mesh):
    tokens = P("segment", ("expert", "dp"), None)
    weight = P("segment", "expert", "dp", None)
    router = P("segment", None, None)
    gain = P("segment", None)
    return jax.shard_map(
        body,
        mesh=mesh,
        in_specs=(tokens, tokens, tokens, tokens, tokens, gain, router, weight, weight, weight),
        out_specs=(tokens, tokens, router, gain),
        check_vma=False,
    )
```

```python
import jax
import jax.numpy as jnp
from jax import lax
from jax.experimental import pallas as pl
from jax.experimental.pallas import tpu as pltpu
from jax.sharding import PartitionSpec as P

EPS = 1e-06
MOST = 8
ROWS_Z = 16
PAIRS = 8
MESH = pl.DeviceIdType.MESH
F32 = jnp.float32
BF16 = jnp.bfloat16


class Place:
    def __init__(self):
        self.seg = lax.axis_index("segment")
        self.exp = lax.axis_index("expert")
        self.dp = lax.axis_index("dp")
        self.y = self.exp // ROWS_Z
        self.z = self.exp % ROWS_Z
        self.zp = self.z // 2
        self.par = self.z % 2
        self.ny = lax.axis_size("expert") // ROWS_Z

    def owner(self, j):
        rel = j % PAIRS
        y = (self.y + j // PAIRS) % self.ny
        zp = (self.zp + rel) % PAIRS
        turn = (rel - self.par + PAIRS) % PAIRS
        exp = y * ROWS_Z + zp * 2 + turn // 4
        return (self.seg, exp, self.dp), y * PAIRS + zp, self.y * PAIRS + self.par * 4 + turn % 4

    def client(self, j):
        r = (7 * self.par + j % PAIRS) % PAIRS
        y = (self.y + j // PAIRS) % self.ny
        par = r // 4
        zp = (self.zp + 2 * PAIRS - (4 * self.par + r % 4 + par)) % PAIRS
        return (self.seg, y * ROWS_Z + zp * 2 + par, self.dp), y * PAIRS + r

    def expert(self):
        return self.y * PAIRS + self.zp

    def core(self):
        return (self.seg, self.exp, 1 - self.dp)

    def twin(self):
        return (self.seg, self.exp + 1 - 2 * self.par, self.dp)


def signal(sem, device):
    pl.semaphore_signal(sem, inc=1, device_id=device, device_id_type=MESH)


def remote(src, dst, send, recv, device):
    return pltpu.make_async_remote_copy(
        src_ref=src, dst_ref=dst, send_sem=send, recv_sem=recv, device_id=device, device_id_type=MESH
    )


def dot(a, b, dims=((1,), (0,))):
    return lax.dot_general(a, b, (dims, ((), ())), preferred_element_type=F32)


def dot_t(a, b):
    return dot(a, b, ((1,), (1,)))


def iota(shape, axis):
    return lax.broadcasted_iota(jnp.int32, shape, axis)


def ones(mask):
    return jnp.where(mask, 1.0, 0.0)


def norm_of(x):
    x_float = x.astype(F32)
    inv_rms = lax.rsqrt(jnp.mean(x_float * x_float, -1, keepdims=True) + EPS)
    return x_float, inv_rms


def columns(route):
    tokens = route.shape[1]
    same = ones(iota((tokens, tokens), 0) == iota((tokens, tokens), 1))
    values = route.astype(F32)
    return [jnp.sum(same * values[k : k + 1, :], -1, keepdims=True).astype(jnp.int32) for k in range(2)]


def prepare(x, route, gain, router_w):
    tokens = x.shape[0]
    experts = router_w.shape[0]
    x_float, inv_rms = norm_of(x)
    normed = (x_float * inv_rms * gain).astype(BF16)
    logits = dot_t(normed, router_w)
    ids = iota((tokens, experts), 1)
    hot = [ones(route[k] == ids) for k in range(2)]
    chosen = [jnp.sum(h * logits, -1, keepdims=True) for h in hot]
    weights = (jax.nn.sigmoid(chosen[0] - chosen[1]), jax.nn.sigmoid(chosen[1] - chosen[0]))
    below = ones(iota((tokens, tokens), 0) > iota((tokens, tokens), 1)).astype(BF16)
    counts = dot(below, (hot[0] + hot[1]).astype(BF16))
    slots = iota((tokens, experts * MOST), 1)
    picks = []
    for k in range(2):
        rank = jnp.sum(hot[k] * counts, -1, keepdims=True).astype(jnp.int32)
        picks.append(ones(route[k] * MOST + rank == slots))
    return normed, weights, picks


def to_slots(both, rows):
    out = dot(both, rows, ((0,), (0,)))
    return out.reshape(out.shape[0] // MOST, MOST, out.shape[1]).astype(BF16)


def flat(blocks):
    return blocks.astype(F32).reshape(blocks.shape[0] * MOST, blocks.shape[2]).astype(BF16)


def kernel(
    act, stash, grad, route_a, route_b, gain, router, wg, wu, wd,
    next_act, prev_grad, router_out, gain_out,
    send_a, send_b, send_g, rec_a, rec_b, rec_g, rows, grads, gate, up, down, acc,
    out_a, out_b, back_a, back_b, normed_b, mixed,
    stash_s, grad_s, picks_b, picks_s, router_s, gain_s, dlog, dlog_s,
    p_send, p_rec, q_send, q_back, rsum, wide, term, held, got, line, total,
    ssem, rsem, own, shift_send, shift_recv, wsend, wrecv, wown, sum_send, sum_recv,
):
    me = Place()
    count = send_a.shape[0]
    tokens = act.shape[0]
    quarters = gate.shape[0]
    width = act.shape[1]
    group = 2 * me.ny
    mine = me.y * 2 + me.dp
    behind, ahead = (me.seg + 3) % 4, (me.seg + 1) % 4
    before = (behind, me.exp, me.dp)
    after = (ahead, me.exp, me.dp)
    barrier = pltpu.get_barrier_semaphore()

    def in_row(o):
        other = (mine + o) % group
        return other, (me.seg, (other // 2) * ROWS_Z + me.z, other % 2)

    def in_column(o):
        other = (me.z + o) % ROWS_Z
        return other, (me.seg, me.y * ROWS_Z + other, me.dp)

    signal(barrier, before)
    signal(barrier, me.core())
    signal(barrier, me.twin())
    signal(barrier, after)

    @pl.loop(1, count)
    def _(j):
        signal(barrier, me.client(j)[0])
        device = me.owner(j)[0]
        signal(barrier, device)
        signal(barrier, (ahead, device[1], device[2]))

    @pl.loop(1, group)
    def _(o):
        signal(barrier, in_row(o)[1])

    @pl.loop(1, ROWS_Z)
    def _(o):
        signal(barrier, in_column(o)[1])

    gain_row = gain[...]
    normed_a, weights_a, picks_a = prepare(act[...], columns(route_a[...]), gain_row, router[...])
    send_a[...] = to_slots((picks_a[0] + picks_a[1]).astype(BF16), normed_a)
    route_cols = columns(route_b[...])
    normed, weights_b, picks = prepare(stash[...], route_cols, gain_row, router[...])
    normed_b[...] = normed
    both = (picks[0] + picks[1]).astype(BF16)
    picks_b[...] = both
    send_b[...] = to_slots(both, normed)
    send_g[...] = to_slots(both, grad[...])
    p_row = jnp.sum(picks[0] * weights_b[0] + picks[1] * weights_b[1], 0, keepdims=True)
    halves = p_send.shape[0]
    for h in range(halves):
        p_send[h] = p_row[:, h * 128 : (h + 1) * 128]
    per_half = count // halves
    pl.semaphore_wait(barrier, 4 + 3 * (count - 1) + group - 1 + ROWS_Z - 1)

    weights = ((wg, gate), (wu, up), (wd, down))

    def to_twin(m):
        return remote(weights[m][0], weights[m][1].at[2], wsend.at[0, m], wrecv.at[0, m], me.twin())

    def to_core(m):
        return remote(weights[m][0], weights[m][1].at[1], wsend.at[1, m], wrecv.at[1, m], me.core())

    def on_to_core(m):
        full = weights[m][1]
        return remote(full.at[2], full.at[3], wsend.at[2, m], wrecv.at[2, m], me.core())

    def to_self(m):
        return pltpu.make_async_copy(weights[m][0], weights[m][1].at[0], wown.at[m])

    def shift(k, src, dst, device):
        return remote(src, dst, shift_send.at[k], shift_recv.at[k], device)

    shifts = [
        shift(0, stash, stash_s, before),
        shift(1, grad, grad_s, before),
        shift(2, router, router_s, before),
        shift(3, gain, gain_s, before),
        shift(4, picks_b, picks_s, before),
        shift(5, dlog, dlog_s, before),
        shift(6, mixed, next_act, after),
    ]

    def send(k, src, dst, block=lambda e: e):
        _, expert, slot = me.owner(0)
        pltpu.make_async_copy(src.at[block(expert)], dst.at[slot], own.at[k]).start()

        @pl.loop(1, count)
        def _(j):
            device, expert, slot = me.owner(j)
            remote(src.at[block(expert)], dst.at[slot], ssem.at[k], rsem.at[k], device).start()

    expert = me.expert()

    def keep_back(k, src, dst):
        pltpu.make_async_copy(src.at[me.client(0)[1]], dst.at[expert], own.at[k]).start()

    def send_back(k, src, dst, first, last):
        @pl.loop(first, last)
        def _(j):
            device, slot = me.client(j)
            remote(src.at[slot], dst.at[expert], ssem.at[k], rsem.at[k], device).start()

    def others(k, ref):
        part = ref.at[pl.ds(0, count - 1)]
        return remote(part, part, ssem.at[k], rsem.at[k], after)

    def arrived(k, ref):
        others(k, ref).wait_recv()
        pltpu.make_async_copy(ref.at[0], ref.at[0], own.at[k]).wait()

    for m in range(3):
        to_twin(m).start()
        to_core(m).start()
        to_self(m).start()
    send(0, send_a, rec_a)
    send(1, send_b, rec_b)
    send(2, send_g, rec_g)
    send(3, p_send, p_rec, lambda e: e // per_half)
    for k in range(5):
        shifts[k].start()

    for m in range(3):
        to_twin(m).wait_recv()
        on_to_core(m).start()
    arrived(0, rec_a)
    rows[...] = flat(rec_a[...])
    for m in range(3):
        to_core(m).wait_recv()
        on_to_core(m).wait_recv()
        to_self(m).wait()
    acc[...] = jnp.zeros_like(acc)

    @pl.loop(0, quarters)
    def _(c):
        gate_val = dot_t(rows[...], gate[c])
        up_val = dot_t(rows[...], up[c])
        hidden = (gate_val * jax.nn.sigmoid(gate_val) * up_val).astype(BF16)
        acc[...] += dot(hidden, down[c])

    out_a[...] = acc[...].reshape(out_a.shape).astype(BF16)
    keep_back(4, out_a, back_a)
    send_back(4, out_a, back_a, 1, count // 2)
    arrived(1, rec_b)
    arrived(2, rec_g)
    arrived(3, p_rec)
    send_back(4, out_a, back_a, count // 2, count)

    rows[...] = flat(rec_b[...])
    grads[...] = flat(rec_g[...])
    acc[...] = jnp.zeros_like(acc)
    slots = count * MOST

    def back_part(c, dots):
        gate_val = dot_t(rows[...], gate[c])
        up_val = dot_t(rows[...], up[c])
        grad_hidden = dot_t(grads[...], down[c])
        sigma = jax.nn.sigmoid(gate_val)
        silu = gate_val * sigma
        hidden = (silu * up_val).astype(BF16)
        grad_gate = (grad_hidden * up_val * sigma * (1.0 + gate_val * (1.0 - sigma))).astype(BF16)
        grad_up = (grad_hidden * silu).astype(BF16)
        acc[...] += dot(grad_gate, gate[c]) + dot(grad_up, up[c])
        return dots + jnp.sum(hidden.astype(F32) * grad_hidden, -1, keepdims=True)

    dots = lax.fori_loop(0, quarters, back_part, jnp.zeros((slots, 1), F32))
    base = (me.expert() % per_half) * MOST
    lanes = ones(iota((count, MOST, 128), 2) == iota((count, MOST, 128), 1) + base)
    q_send[...] = jnp.sum(lanes * dots.reshape(count, MOST, 1), 1, keepdims=True)
    keep_back(5, q_send, q_back)
    send_back(5, q_send, q_back, 1, count)
    p_col = jnp.sum(lanes * p_rec[...], 2, keepdims=True).reshape(slots, 1)
    scaled = acc[...] * p_col
    out_b[...] = scaled.reshape(out_b.shape).astype(BF16)

    def grads_back(part):
        cuts = (0, 12, 20, 28, count)

        @pl.loop(cuts[part], cuts[part + 1])
        def _(j):
            device, slot = me.client(j)
            device = (behind, device[1], device[2])
            remote(out_b.at[slot], back_b.at[expert], ssem.at[6], rsem.at[6], device).start()

    grads_back(0)
    gain_own = jnp.sum(scaled * rows[...].astype(F32), 0, keepdims=True) / gain_row

    arrived(5, q_back)
    q_all = q_back[...]
    q_row = jnp.concatenate(
        [jnp.sum(q_all[h * per_half : (h + 1) * per_half], 0) for h in range(halves)], 1
    )
    dot_of = [jnp.sum(pick * q_row, -1, keepdims=True) for pick in picks]
    logit_grad = weights_b[0] * weights_b[1] * (dot_of[0] - dot_of[1])
    ids = iota((tokens, 128), 1)
    signs = ones(route_cols[0] == ids) - ones(route_cols[1] == ids)
    dlogits = (logit_grad * signs).astype(BF16)
    dlog[...] = dlogits
    shifts[5].start()
    x_float, inv_rms = norm_of(stash[...])
    dlogits = dlogits[:, :count]
    rsum[...] = dot(dlogits, normed_b[...], ((0,), (0,)))
    gain_part = gain_own + jnp.sum(dot(dlogits, router[...]) * x_float * inv_rms, 0, keepdims=True)
    per = count // group
    wide[...] = jnp.zeros_like(wide)
    for g in range(group):
        for c in range(ROWS_Z):
            wide[g, c, 0:per, :] = rsum[g * per : (g + 1) * per, c * 128 : (c + 1) * 128]
    for c in range(ROWS_Z):
        wide[0, c, per : per + 1, :] = gain_part[:, c * 128 : (c + 1) * 128]
    term[...] = wide[...].astype(BF16)

    @pl.loop(1, group)
    def _(o):
        other, device = in_row(o)
        remote(term.at[other], got.at[o - 1], sum_send.at[0], sum_recv.at[0], device).start()

    def summed(k, ref):
        return remote(ref, ref, sum_send.at[k], sum_recv.at[k], after)

    grads_back(1)
    summed(0, got).wait_recv()
    held[...] = (wide[mine] + jnp.sum(got[...].astype(F32), 0)).astype(BF16)

    @pl.loop(1, ROWS_Z)
    def _(o):
        other, device = in_column(o)
        remote(held.at[other], line.at[o - 1], sum_send.at[1], sum_recv.at[1], device).start()

    grads_back(2)
    summed(1, line).wait_recv()
    total[mine, me.z] = (held[me.z].astype(F32) + jnp.sum(line[...].astype(F32), 0)).astype(BF16)

    @pl.loop(1, ROWS_Z)
    def _(o):
        here = total.at[mine, me.z]
        remote(here, here, sum_send.at[2], sum_recv.at[2], in_column(o)[1]).start()

    grads_back(3)
    summed(2, line).wait_recv()

    @pl.loop(1, group)
    def _(o):
        remote(total.at[mine], total.at[mine], sum_send.at[3], sum_recv.at[3], in_row(o)[1]).start()

    arrived(4, back_a)
    returned = flat(back_a[...])
    mixed[...] = (
        act[...].astype(F32)
        + weights_a[0] * dot(picks_a[0].astype(BF16), returned)
        + weights_a[1] * dot(picks_a[1].astype(BF16), returned)
    ).astype(BF16)
    shifts[6].start()

    summed(3, got).wait_recv()
    scale = 1.0 / (group * ROWS_Z)
    wide[...] = total[...].astype(F32) * scale
    for g in range(group):
        for c in range(ROWS_Z):
            router_out[g * per : (g + 1) * per, c * 128 : (c + 1) * 128] = wide[g, c, 0:per, :]
    for c in range(ROWS_Z):
        gain_out[:, c * 128 : (c + 1) * 128] = wide[0, c, per : per + 1, :]

    for k in range(6):
        shifts[k].wait_recv()
    x_float, inv_rms = norm_of(stash_s[...])
    acc[0:tokens, :] = dot(dlog_s[...][:, :count], router_s[...])
    remote(out_b, back_b, ssem.at[6], rsem.at[6], after).wait_recv()
    dnormed = acc[0:tokens, :] + dot(picks_s[...], flat(back_b[...]))
    dxn = dnormed * gain_s[...]
    prev_grad[...] = (
        grad_s[...].astype(F32)
        + inv_rms * dxn
        - x_float * (inv_rms * inv_rms * inv_rms * jnp.mean(dxn * x_float, -1, keepdims=True))
    ).astype(BF16)

    for m in range(3):
        to_twin(m).wait_send()
        to_core(m).wait_send()
        on_to_core(m).wait_send()
    for k, ref in enumerate((rec_a, rec_b, rec_g, p_rec, back_a, q_back)):
        others(k, ref).wait_send()
    remote(out_b, back_b, ssem.at[6], rsem.at[6], after).wait_send()
    for k in range(7):
        shifts[k].wait_send()
    shifts[6].wait_recv()
    for k, ref in enumerate((got, line, line, got)):
        summed(k, ref).wait_send()


HBM = pl.BlockSpec(memory_space=pltpu.HBM)
VMEM = pl.BlockSpec(memory_space=pltpu.VMEM)


def like(shape, dtype):
    return jax.ShapeDtypeStruct(shape, dtype)


def body(
    act_in, stash_in, grad_in, route_a, route_b, norm_gain, router, gate_weight, up_weight, down_weight
):
    tokens, width = act_in.shape[1:]
    experts = router.shape[1]
    quarter = gate_weight.shape[2]
    group = lax.axis_size("expert") * lax.axis_size("dp") // ROWS_Z
    slots = experts * MOST
    block = (experts, MOST, width)
    dma = pltpu.SemaphoreType.DMA

    def vb(*shape):
        return pltpu.VMEM(shape, BF16)

    def vf(*shape):
        return pltpu.VMEM(shape, F32)

    full = vb(4, quarter, width)
    row = (tokens, width)
    lanes = (experts, 1, 128)
    next_act, prev_grad, router_grad, gain_grad = pl.pallas_call(
        kernel,
        out_shape=[like(row, BF16), like(row, BF16), like((experts, width), F32), like((1, width), F32)],
        in_specs=[VMEM] * 7 + [HBM] * 3,
        out_specs=[VMEM] * 4,
        scratch_shapes=[vb(*block)] * 6
        + [vb(slots, width)] * 2
        + [full] * 3
        + [vf(slots, width)]
        + [vb(*block)] * 4
        + [vb(*row)] * 2
        + [vb(*row)] * 2
        + [vb(tokens, slots)] * 2
        + [vb(experts, width), vf(1, width)]
        + [vb(tokens, 128)] * 2
        + [vf(slots // 128, 1, 128), vf(*lanes), vf(*lanes), vf(*lanes)]
        + [vf(experts, width), vf(group, ROWS_Z, 8, 128), vb(group, ROWS_Z, 8, 128), vb(ROWS_Z, 8, 128)]
        + [vb(group - 1, ROWS_Z, 8, 128), vb(ROWS_Z - 1, 8, 128), vb(group, ROWS_Z, 8, 128)]
        + [dma((7,)), dma((7,)), dma((6,)), dma((7,)), dma((7,))]
        + [dma((3, 3)), dma((3, 3)), dma((3,)), dma((4,)), dma((4,))],
        compiler_params=pltpu.CompilerParams(
            collective_id=0, has_side_effects=True, vmem_limit_bytes=40 << 20
        ),
    )(
        act_in[0], stash_in[0], grad_in[0], route_a[0].T, route_b[0].T, norm_gain, router[0],
        gate_weight[0, 0], up_weight[0, 0], down_weight[0, 0],
    )
    return next_act[None], prev_grad[None], router_grad[None], gain_grad


def solution(mesh):
    tokens = P("segment", ("expert", "dp"), None)
    weight = P("segment", "expert", "dp", None)
    router = P("segment", None, None)
    gain = P("segment", None)
    return jax.shard_map(
        body,
        mesh=mesh,
        in_specs=(tokens, tokens, tokens, tokens, tokens, gain, router, weight, weight, weight),
        out_specs=(tokens, tokens, router, gain),
        check_vma=False,
    )
```

```python
import jax
import jax.numpy as jnp
from jax import lax
from jax.experimental import pallas as pl
from jax.experimental.pallas import tpu as pltpu
from jax.sharding import PartitionSpec as P

EPS = 1e-06
MOST = 8
ROWS_Z = 16
PAIRS = 8
MESH = pl.DeviceIdType.MESH
F32 = jnp.float32
BF16 = jnp.bfloat16


class Place:
    def __init__(self):
        self.seg = lax.axis_index("segment")
        self.exp = lax.axis_index("expert")
        self.dp = lax.axis_index("dp")
        self.y = self.exp // ROWS_Z
        self.z = self.exp % ROWS_Z
        self.zp = self.z // 2
        self.par = self.z % 2
        self.ny = lax.axis_size("expert") // ROWS_Z

    def owner(self, j):
        rel = j % PAIRS
        y = (self.y + j // PAIRS) % self.ny
        zp = (self.zp + rel) % PAIRS
        turn = (rel - self.par + PAIRS) % PAIRS
        exp = y * ROWS_Z + zp * 2 + turn // 4
        return (self.seg, exp, self.dp), y * PAIRS + zp, self.y * PAIRS + self.par * 4 + turn % 4

    def client(self, j):
        r = (7 * self.par + j % PAIRS) % PAIRS
        y = (self.y + j // PAIRS) % self.ny
        par = r // 4
        zp = (self.zp + 2 * PAIRS - (4 * self.par + r % 4 + par)) % PAIRS
        return (self.seg, y * ROWS_Z + zp * 2 + par, self.dp), y * PAIRS + r

    def expert(self):
        return self.y * PAIRS + self.zp

    def core(self):
        return (self.seg, self.exp, 1 - self.dp)

    def twin(self):
        return (self.seg, self.exp + 1 - 2 * self.par, self.dp)


def signal(sem, device):
    pl.semaphore_signal(sem, inc=1, device_id=device, device_id_type=MESH)


def remote(src, dst, send, recv, device):
    return pltpu.make_async_remote_copy(
        src_ref=src, dst_ref=dst, send_sem=send, recv_sem=recv, device_id=device, device_id_type=MESH
    )


def dot(a, b, dims=((1,), (0,))):
    return lax.dot_general(a, b, (dims, ((), ())), preferred_element_type=F32)


def dot_t(a, b):
    return dot(a, b, ((1,), (1,)))


def iota(shape, axis):
    return lax.broadcasted_iota(jnp.int32, shape, axis)


def ones(mask):
    return jnp.where(mask, 1.0, 0.0)


def norm_of(x):
    x_float = x.astype(F32)
    inv_rms = lax.rsqrt(jnp.mean(x_float * x_float, -1, keepdims=True) + EPS)
    return x_float, inv_rms


def columns(route):
    tokens = route.shape[1]
    same = ones(iota((tokens, tokens), 0) == iota((tokens, tokens), 1))
    values = route.astype(F32)
    return [jnp.sum(same * values[k : k + 1, :], -1, keepdims=True).astype(jnp.int32) for k in range(2)]


def choose(route, experts):
    tokens = route[0].shape[0]
    ids = iota((tokens, experts), 1)
    hot = [ones(r == ids) for r in route]
    below = ones(iota((tokens, tokens), 0) > iota((tokens, tokens), 1)).astype(BF16)
    counts = dot(below, (hot[0] + hot[1]).astype(BF16))
    slots = iota((tokens, experts * MOST), 1)
    picks = []
    for k in range(2):
        rank = jnp.sum(hot[k] * counts, -1, keepdims=True).astype(jnp.int32)
        picks.append(ones(route[k] * MOST + rank == slots))
    return hot, picks


def prepare(x, hot, gain, router_w):
    x_float, inv_rms = norm_of(x)
    normed = (x_float * inv_rms * gain).astype(BF16)
    logits = dot_t(normed, router_w)
    chosen = [jnp.sum(h * logits, -1, keepdims=True) for h in hot]
    return normed, (jax.nn.sigmoid(chosen[0] - chosen[1]), jax.nn.sigmoid(chosen[1] - chosen[0]))


def to_slots(both, rows):
    out = dot(both, rows, ((0,), (0,)))
    return out.reshape(out.shape[0] // MOST, MOST, out.shape[1]).astype(BF16)


def flat(blocks):
    return blocks.astype(F32).reshape(blocks.shape[0] * MOST, blocks.shape[2]).astype(BF16)


def kernel(
    act, stash, grad, route_a, route_b, gain, router, wg, wu, wd,
    next_act, prev_grad, router_out, gain_out,
    send_a, send_b, send_g, rec_a, rec_b, rec_g, rows, grads, gate, up, down, acc,
    out_a, out_b, back_a, back_b, normed_b, mixed,
    stash_s, grad_s, picks_b, picks_s, router_s, gain_s, dlog, dlog_s,
    p_send, p_rec, q_send, q_back, rsum, wide, term, held, got, line, total,
    ssem, rsem, own, shift_send, shift_recv, wsend, wrecv, wown, sum_send, sum_recv,
):
    me = Place()
    count = send_a.shape[0]
    tokens = act.shape[0]
    quarters = gate.shape[0]
    width = act.shape[1]
    group = 2 * me.ny
    mine = me.y * 2 + me.dp
    behind, ahead = (me.seg + 3) % 4, (me.seg + 1) % 4
    before = (behind, me.exp, me.dp)
    after = (ahead, me.exp, me.dp)
    barrier = pltpu.get_barrier_semaphore()

    def in_row(o):
        other = (mine + o) % group
        return other, (me.seg, (other // 2) * ROWS_Z + me.z, other % 2)

    def in_column(o):
        other = (me.z + o) % ROWS_Z
        return other, (me.seg, me.y * ROWS_Z + other, me.dp)

    signal(barrier, before)
    signal(barrier, me.core())
    signal(barrier, me.twin())
    signal(barrier, after)

    @pl.loop(1, count)
    def _(j):
        signal(barrier, me.client(j)[0])
        device = me.owner(j)[0]
        signal(barrier, device)
        signal(barrier, (ahead, device[1], device[2]))

    @pl.loop(1, group)
    def _(o):
        signal(barrier, in_row(o)[1])

    @pl.loop(1, ROWS_Z)
    def _(o):
        signal(barrier, in_column(o)[1])

    pl.semaphore_wait(barrier, 4 + 3 * (count - 1) + group - 1 + ROWS_Z - 1)

    weights = ((wg, gate), (wu, up), (wd, down))

    def to_twin(m):
        return remote(weights[m][0], weights[m][1].at[2], wsend.at[0, m], wrecv.at[0, m], me.twin())

    def to_core(m):
        return remote(weights[m][0], weights[m][1].at[1], wsend.at[1, m], wrecv.at[1, m], me.core())

    def on_to_core(m):
        full = weights[m][1]
        return remote(full.at[2], full.at[3], wsend.at[2, m], wrecv.at[2, m], me.core())

    def to_self(m):
        return pltpu.make_async_copy(weights[m][0], weights[m][1].at[0], wown.at[m])

    def shift(k, src, dst, device):
        return remote(src, dst, shift_send.at[k], shift_recv.at[k], device)

    shifts = [
        shift(0, stash, stash_s, before),
        shift(1, grad, grad_s, before),
        shift(2, router, router_s, before),
        shift(3, gain, gain_s, before),
        shift(4, picks_b, picks_s, before),
        shift(5, dlog, dlog_s, before),
        shift(6, mixed, next_act, after),
    ]

    def send(k, src, dst, block=lambda e: e):
        _, expert, slot = me.owner(0)
        pltpu.make_async_copy(src.at[block(expert)], dst.at[slot], own.at[k]).start()

        @pl.loop(1, count)
        def _(j):
            device, expert, slot = me.owner(j)
            remote(src.at[block(expert)], dst.at[slot], ssem.at[k], rsem.at[k], device).start()

    expert = me.expert()

    def keep_back(k, src, dst):
        pltpu.make_async_copy(src.at[me.client(0)[1]], dst.at[expert], own.at[k]).start()

    def send_back(k, src, dst, first, last):
        @pl.loop(first, last)
        def _(j):
            device, slot = me.client(j)
            remote(src.at[slot], dst.at[expert], ssem.at[k], rsem.at[k], device).start()

    def others(k, ref):
        part = ref.at[pl.ds(0, count - 1)]
        return remote(part, part, ssem.at[k], rsem.at[k], after)

    def arrived(k, ref):
        others(k, ref).wait_recv()
        pltpu.make_async_copy(ref.at[0], ref.at[0], own.at[k]).wait()

    for m in range(3):
        to_twin(m).start()
        to_core(m).start()
        to_self(m).start()
    gain_row = gain[...]
    route_cols = columns(route_b[...])
    hot, picks = choose(route_cols, count)
    both = (picks[0] + picks[1]).astype(BF16)
    send_g[...] = to_slots(both, grad[...])
    send(2, send_g, rec_g)
    normed, weights_b = prepare(stash[...], hot, gain_row, router[...])
    send_b[...] = to_slots(both, normed)
    send(1, send_b, rec_b)
    hot_a, picks_a = choose(columns(route_a[...]), count)
    normed_a, weights_a = prepare(act[...], hot_a, gain_row, router[...])
    send_a[...] = to_slots((picks_a[0] + picks_a[1]).astype(BF16), normed_a)
    send(0, send_a, rec_a)
    normed_b[...] = normed
    picks_b[...] = both
    for k in range(5):
        shifts[k].start()
    p_row = jnp.sum(picks[0] * weights_b[0] + picks[1] * weights_b[1], 0, keepdims=True)
    halves = p_send.shape[0]
    for h in range(halves):
        p_send[h] = p_row[:, h * 128 : (h + 1) * 128]
    per_half = count // halves
    send(3, p_send, p_rec, lambda e: e // per_half)

    for m in range(3):
        to_twin(m).wait_recv()
        on_to_core(m).start()
    arrived(0, rec_a)
    rows[...] = flat(rec_a[...])
    for m in range(3):
        to_core(m).wait_recv()
        on_to_core(m).wait_recv()
        to_self(m).wait()
    acc[...] = jnp.zeros_like(acc)

    @pl.loop(0, quarters)
    def _(c):
        gate_val = dot_t(rows[...], gate[c])
        up_val = dot_t(rows[...], up[c])
        hidden = (gate_val * jax.nn.sigmoid(gate_val) * up_val).astype(BF16)
        acc[...] += dot(hidden, down[c])

    out_a[...] = acc[...].reshape(out_a.shape).astype(BF16)
    keep_back(4, out_a, back_a)
    send_back(4, out_a, back_a, 1, count * 5 // 8)
    arrived(1, rec_b)
    arrived(2, rec_g)
    arrived(3, p_rec)
    send_back(4, out_a, back_a, count * 5 // 8, count)

    rows[...] = flat(rec_b[...])
    grads[...] = flat(rec_g[...])
    acc[...] = jnp.zeros_like(acc)
    slots = count * MOST

    def back_part(c, dots):
        gate_val = dot_t(rows[...], gate[c])
        up_val = dot_t(rows[...], up[c])
        grad_hidden = dot_t(grads[...], down[c])
        sigma = jax.nn.sigmoid(gate_val)
        silu = gate_val * sigma
        hidden = (silu * up_val).astype(BF16)
        grad_gate = (grad_hidden * up_val * sigma * (1.0 + gate_val * (1.0 - sigma))).astype(BF16)
        grad_up = (grad_hidden * silu).astype(BF16)
        acc[...] += dot(grad_gate, gate[c]) + dot(grad_up, up[c])
        return dots + jnp.sum(hidden.astype(F32) * grad_hidden, -1, keepdims=True)

    dots = lax.fori_loop(0, quarters, back_part, jnp.zeros((slots, 1), F32))
    base = (me.expert() % per_half) * MOST
    lanes = ones(iota((count, MOST, 128), 2) == iota((count, MOST, 128), 1) + base)
    q_send[...] = jnp.sum(lanes * dots.reshape(count, MOST, 1), 1, keepdims=True)
    keep_back(5, q_send, q_back)
    send_back(5, q_send, q_back, 1, count)
    p_col = jnp.sum(lanes * p_rec[...], 2, keepdims=True).reshape(slots, 1)
    scaled = acc[...] * p_col
    out_b[...] = scaled.reshape(out_b.shape).astype(BF16)

    def grads_back(part):
        @pl.loop(part * count // 4, (part + 1) * count // 4)
        def _(j):
            device, slot = me.client(j)
            device = (behind, device[1], device[2])
            remote(out_b.at[slot], back_b.at[expert], ssem.at[6], rsem.at[6], device).start()

    grads_back(0)
    gain_own = jnp.sum(scaled * rows[...].astype(F32), 0, keepdims=True) / gain_row

    arrived(5, q_back)
    q_all = q_back[...]
    q_row = jnp.concatenate(
        [jnp.sum(q_all[h * per_half : (h + 1) * per_half], 0) for h in range(halves)], 1
    )
    dot_of = [jnp.sum(pick * q_row, -1, keepdims=True) for pick in picks]
    logit_grad = weights_b[0] * weights_b[1] * (dot_of[0] - dot_of[1])
    ids = iota((tokens, 128), 1)
    signs = ones(route_cols[0] == ids) - ones(route_cols[1] == ids)
    dlogits = (logit_grad * signs).astype(BF16)
    dlog[...] = dlogits
    shifts[5].start()
    x_float, inv_rms = norm_of(stash[...])
    dlogits = dlogits[:, :count]
    rsum[...] = dot(dlogits, normed_b[...], ((0,), (0,)))
    gain_part = gain_own + jnp.sum(dot(dlogits, router[...]) * x_float * inv_rms, 0, keepdims=True)
    per = count // group
    wide[...] = jnp.zeros_like(wide)
    for g in range(group):
        for c in range(ROWS_Z):
            wide[g, c, 0:per, :] = rsum[g * per : (g + 1) * per, c * 128 : (c + 1) * 128]
    for c in range(ROWS_Z):
        wide[0, c, per : per + 1, :] = gain_part[:, c * 128 : (c + 1) * 128]
    term[...] = wide[...].astype(BF16)

    @pl.loop(1, group)
    def _(o):
        other, device = in_row(o)
        remote(term.at[other], got.at[o - 1], sum_send.at[0], sum_recv.at[0], device).start()

    def summed(k, ref):
        return remote(ref, ref, sum_send.at[k], sum_recv.at[k], after)

    grads_back(1)
    summed(0, got).wait_recv()
    held[...] = (wide[mine] + jnp.sum(got[...].astype(F32), 0)).astype(BF16)

    @pl.loop(1, ROWS_Z)
    def _(o):
        other, device = in_column(o)
        remote(held.at[other], line.at[o - 1], sum_send.at[1], sum_recv.at[1], device).start()

    grads_back(2)
    summed(1, line).wait_recv()
    total[mine, me.z] = (held[me.z].astype(F32) + jnp.sum(line[...].astype(F32), 0)).astype(BF16)

    @pl.loop(1, ROWS_Z)
    def _(o):
        here = total.at[mine, me.z]
        remote(here, here, sum_send.at[2], sum_recv.at[2], in_column(o)[1]).start()

    grads_back(3)
    summed(2, line).wait_recv()

    @pl.loop(1, group)
    def _(o):
        remote(total.at[mine], total.at[mine], sum_send.at[3], sum_recv.at[3], in_row(o)[1]).start()

    arrived(4, back_a)
    returned = flat(back_a[...])
    mixed[...] = (
        act[...].astype(F32)
        + weights_a[0] * dot(picks_a[0].astype(BF16), returned)
        + weights_a[1] * dot(picks_a[1].astype(BF16), returned)
    ).astype(BF16)
    shifts[6].start()

    summed(3, got).wait_recv()
    scale = 1.0 / (group * ROWS_Z)
    wide[...] = total[...].astype(F32) * scale
    for g in range(group):
        for c in range(ROWS_Z):
            router_out[g * per : (g + 1) * per, c * 128 : (c + 1) * 128] = wide[g, c, 0:per, :]
    for c in range(ROWS_Z):
        gain_out[:, c * 128 : (c + 1) * 128] = wide[0, c, per : per + 1, :]

    for k in range(6):
        shifts[k].wait_recv()
    x_float, inv_rms = norm_of(stash_s[...])
    acc[0:tokens, :] = dot(dlog_s[...][:, :count], router_s[...])
    remote(out_b, back_b, ssem.at[6], rsem.at[6], after).wait_recv()
    dnormed = acc[0:tokens, :] + dot(picks_s[...], flat(back_b[...]))
    dxn = dnormed * gain_s[...]
    prev_grad[...] = (
        grad_s[...].astype(F32)
        + inv_rms * dxn
        - x_float * (inv_rms * inv_rms * inv_rms * jnp.mean(dxn * x_float, -1, keepdims=True))
    ).astype(BF16)

    for m in range(3):
        to_twin(m).wait_send()
        to_core(m).wait_send()
        on_to_core(m).wait_send()
    for k, ref in enumerate((rec_a, rec_b, rec_g, p_rec, back_a, q_back)):
        others(k, ref).wait_send()
    remote(out_b, back_b, ssem.at[6], rsem.at[6], after).wait_send()
    for k in range(7):
        shifts[k].wait_send()
    shifts[6].wait_recv()
    for k, ref in enumerate((got, line, line, got)):
        summed(k, ref).wait_send()


ANY = pl.BlockSpec(memory_space=pl.ANY)
VMEM = pl.BlockSpec(memory_space=pltpu.VMEM)


def like(shape, dtype):
    return jax.ShapeDtypeStruct(shape, dtype)


def body(
    act_in, stash_in, grad_in, route_a, route_b, norm_gain, router, gate_weight, up_weight, down_weight
):
    tokens, width = act_in.shape[1:]
    experts = router.shape[1]
    quarter = gate_weight.shape[2]
    group = lax.axis_size("expert") * lax.axis_size("dp") // ROWS_Z
    slots = experts * MOST
    block = (experts, MOST, width)
    dma = pltpu.SemaphoreType.DMA

    def vb(*shape):
        return pltpu.VMEM(shape, BF16)

    def vf(*shape):
        return pltpu.VMEM(shape, F32)

    full = vb(4, quarter, width)
    row = (tokens, width)
    lanes = (experts, 1, 128)
    next_act, prev_grad, router_grad, gain_grad = pl.pallas_call(
        kernel,
        out_shape=[like(row, BF16), like(row, BF16), like((experts, width), F32), like((1, width), F32)],
        in_specs=[VMEM] * 7 + [ANY] * 3,
        out_specs=[VMEM] * 4,
        scratch_shapes=[vb(*block)] * 6
        + [vb(slots, width)] * 2
        + [full] * 3
        + [vf(slots, width)]
        + [vb(*block)] * 4
        + [vb(*row)] * 2
        + [vb(*row)] * 2
        + [vb(tokens, slots)] * 2
        + [vb(experts, width), vf(1, width)]
        + [vb(tokens, 128)] * 2
        + [vf(slots // 128, 1, 128), vf(*lanes), vf(*lanes), vf(*lanes)]
        + [vf(experts, width), vf(group, ROWS_Z, 8, 128), vb(group, ROWS_Z, 8, 128), vb(ROWS_Z, 8, 128)]
        + [vb(group - 1, ROWS_Z, 8, 128), vb(ROWS_Z - 1, 8, 128), vb(group, ROWS_Z, 8, 128)]
        + [dma((7,)), dma((7,)), dma((6,)), dma((7,)), dma((7,))]
        + [dma((3, 3)), dma((3, 3)), dma((3,)), dma((4,)), dma((4,))],
        compiler_params=pltpu.CompilerParams(
            collective_id=0, has_side_effects=True, vmem_limit_bytes=56 << 20
        ),
    )(
        act_in[0], stash_in[0], grad_in[0], route_a[0].T, route_b[0].T, norm_gain, router[0],
        gate_weight[0, 0], up_weight[0, 0], down_weight[0, 0],
    )
    return next_act[None], prev_grad[None], router_grad[None], gain_grad


def solution(mesh):
    tokens = P("segment", ("expert", "dp"), None)
    weight = P("segment", "expert", "dp", None)
    router = P("segment", None, None)
    gain = P("segment", None)
    return jax.shard_map(
        body,
        mesh=mesh,
        in_specs=(tokens, tokens, tokens, tokens, tokens, gain, router, weight, weight, weight),
        out_specs=(tokens, tokens, router, gain),
        check_vma=False,
    )
```

```python
import jax
import jax.numpy as jnp
from jax import lax
from jax.experimental import pallas as pl
from jax.experimental.pallas import tpu as pltpu
from jax.sharding import PartitionSpec as P

EPS = 1e-06
MOST = 8
ROWS_Z = 16
PAIRS = 8
MESH = pl.DeviceIdType.MESH
F32 = jnp.float32
BF16 = jnp.bfloat16


class Place:
    def __init__(self):
        self.seg = lax.axis_index("segment")
        self.exp = lax.axis_index("expert")
        self.dp = lax.axis_index("dp")
        self.y = self.exp // ROWS_Z
        self.z = self.exp % ROWS_Z
        self.zp = self.z // 2
        self.par = self.z % 2
        self.ny = lax.axis_size("expert") // ROWS_Z

    def owner(self, j):
        rel = j % PAIRS
        y = (self.y + j // PAIRS) % self.ny
        zp = (self.zp + rel) % PAIRS
        turn = (rel - self.par + PAIRS) % PAIRS
        exp = y * ROWS_Z + zp * 2 + turn // 4
        return (self.seg, exp, self.dp), y * PAIRS + zp, self.y * PAIRS + self.par * 4 + turn % 4

    def client(self, j):
        r = (7 * self.par + j % PAIRS) % PAIRS
        y = (self.y + j // PAIRS) % self.ny
        par = r // 4
        zp = (self.zp + 2 * PAIRS - (4 * self.par + r % 4 + par)) % PAIRS
        return (self.seg, y * ROWS_Z + zp * 2 + par, self.dp), y * PAIRS + r

    def expert(self):
        return self.y * PAIRS + self.zp

    def core(self):
        return (self.seg, self.exp, 1 - self.dp)

    def twin(self):
        return (self.seg, self.exp + 1 - 2 * self.par, self.dp)


def signal(sem, device):
    pl.semaphore_signal(sem, inc=1, device_id=device, device_id_type=MESH)


def remote(src, dst, send, recv, device):
    return pltpu.make_async_remote_copy(
        src_ref=src, dst_ref=dst, send_sem=send, recv_sem=recv, device_id=device, device_id_type=MESH
    )


def dot(a, b, dims=((1,), (0,))):
    return lax.dot_general(a, b, (dims, ((), ())), preferred_element_type=F32)


def dot_t(a, b):
    return dot(a, b, ((1,), (1,)))


def iota(shape, axis):
    return lax.broadcasted_iota(jnp.int32, shape, axis)


def ones(mask):
    return jnp.where(mask, 1.0, 0.0)


def norm_of(x):
    x_float = x.astype(F32)
    inv_rms = lax.rsqrt(jnp.mean(x_float * x_float, -1, keepdims=True) + EPS)
    return x_float, inv_rms


def columns(route):
    tokens = route.shape[1]
    same = ones(iota((tokens, tokens), 0) == iota((tokens, tokens), 1))
    values = route.astype(F32)
    return [jnp.sum(same * values[k : k + 1, :], -1, keepdims=True).astype(jnp.int32) for k in range(2)]


def prepare(x, route, gain, router_w):
    tokens = x.shape[0]
    experts = router_w.shape[0]
    x_float, inv_rms = norm_of(x)
    normed = (x_float * inv_rms * gain).astype(BF16)
    logits = dot_t(normed, router_w)
    ids = iota((tokens, experts), 1)
    hot = [ones(route[k] == ids) for k in range(2)]
    chosen = [jnp.sum(h * logits, -1, keepdims=True) for h in hot]
    weights = (jax.nn.sigmoid(chosen[0] - chosen[1]), jax.nn.sigmoid(chosen[1] - chosen[0]))
    below = ones(iota((tokens, tokens), 0) > iota((tokens, tokens), 1)).astype(BF16)
    counts = dot(below, (hot[0] + hot[1]).astype(BF16))
    slots = iota((tokens, experts * MOST), 1)
    picks = []
    for k in range(2):
        rank = jnp.sum(hot[k] * counts, -1, keepdims=True).astype(jnp.int32)
        picks.append(ones(route[k] * MOST + rank == slots))
    return normed, weights, picks


def to_slots(both, rows):
    out = dot(both, rows, ((0,), (0,)))
    return out.reshape(out.shape[0] // MOST, MOST, out.shape[1]).astype(BF16)


def flat(blocks):
    return blocks.astype(F32).reshape(blocks.shape[0] * MOST, blocks.shape[2]).astype(BF16)


def kernel(
    act, stash, grad, route_a, route_b, gain, router, wg, wu, wd,
    next_act, prev_grad, router_out, gain_out,
    send_a, send_b, send_g, rec_a, rec_b, rec_g, rows, grads, gate, up, down, acc,
    out_a, out_b, back_a, back_b, normed_b, mixed,
    stash_s, grad_s, picks_b, picks_s, router_s, gain_s, dlog, dlog_s,
    p_send, p_rec, q_send, q_back, rsum, wide, term, held, got, line, total,
    ssem, rsem, own, shift_send, shift_recv, wsend, wrecv, wown, sum_send, sum_recv,
):
    me = Place()
    count = send_a.shape[0]
    tokens = act.shape[0]
    quarters = gate.shape[0]
    width = act.shape[1]
    group = 2 * me.ny
    mine = me.y * 2 + me.dp
    behind, ahead = (me.seg + 3) % 4, (me.seg + 1) % 4
    before = (behind, me.exp, me.dp)
    after = (ahead, me.exp, me.dp)
    barrier = pltpu.get_barrier_semaphore()

    def in_row(o):
        other = (mine + o) % group
        return other, (me.seg, (other // 2) * ROWS_Z + me.z, other % 2)

    def in_column(o):
        other = (me.z + o) % ROWS_Z
        return other, (me.seg, me.y * ROWS_Z + other, me.dp)

    signal(barrier, before)
    signal(barrier, me.core())
    signal(barrier, me.twin())
    signal(barrier, after)

    @pl.loop(1, count)
    def _(j):
        signal(barrier, me.client(j)[0])
        device = me.owner(j)[0]
        signal(barrier, device)
        signal(barrier, (ahead, device[1], device[2]))

    @pl.loop(1, group)
    def _(o):
        signal(barrier, in_row(o)[1])

    @pl.loop(1, ROWS_Z)
    def _(o):
        signal(barrier, in_column(o)[1])

    pl.semaphore_wait(barrier, 4 + 3 * (count - 1) + group - 1 + ROWS_Z - 1)

    weights = ((wg, gate), (wu, up), (wd, down))

    def to_twin(m):
        return remote(weights[m][0], weights[m][1].at[2], wsend.at[0, m], wrecv.at[0, m], me.twin())

    def to_core(m):
        return remote(weights[m][0], weights[m][1].at[1], wsend.at[1, m], wrecv.at[1, m], me.core())

    def on_to_core(m):
        full = weights[m][1]
        return remote(full.at[2], full.at[3], wsend.at[2, m], wrecv.at[2, m], me.core())

    def to_self(m):
        return pltpu.make_async_copy(weights[m][0], weights[m][1].at[0], wown.at[m])

    def shift(k, src, dst, device):
        return remote(src, dst, shift_send.at[k], shift_recv.at[k], device)

    shifts = [
        shift(0, stash, stash_s, before),
        shift(1, grad, grad_s, before),
        shift(2, router, router_s, before),
        shift(3, gain, gain_s, before),
        shift(4, picks_b, picks_s, before),
        shift(5, dlog, dlog_s, before),
        shift(6, mixed, next_act, after),
    ]

    def send(k, src, dst, block=lambda e: e):
        _, expert, slot = me.owner(0)
        pltpu.make_async_copy(src.at[block(expert)], dst.at[slot], own.at[k]).start()

        @pl.loop(1, count)
        def _(j):
            device, expert, slot = me.owner(j)
            remote(src.at[block(expert)], dst.at[slot], ssem.at[k], rsem.at[k], device).start()

    expert = me.expert()

    def keep_back(k, src, dst):
        pltpu.make_async_copy(src.at[me.client(0)[1]], dst.at[expert], own.at[k]).start()

    def send_back(k, src, dst, first, last):
        @pl.loop(first, last)
        def _(j):
            device, slot = me.client(j)
            remote(src.at[slot], dst.at[expert], ssem.at[k], rsem.at[k], device).start()

    def others(k, ref):
        part = ref.at[pl.ds(0, count - 1)]
        return remote(part, part, ssem.at[k], rsem.at[k], after)

    def arrived(k, ref):
        others(k, ref).wait_recv()
        pltpu.make_async_copy(ref.at[0], ref.at[0], own.at[k]).wait()

    for m in range(3):
        to_twin(m).start()
        to_core(m).start()
        to_self(m).start()
    gain_row = gain[...]
    normed_a, weights_a, picks_a = prepare(act[...], columns(route_a[...]), gain_row, router[...])
    send_a[...] = to_slots((picks_a[0] + picks_a[1]).astype(BF16), normed_a)
    send(0, send_a, rec_a)

    route_cols = columns(route_b[...])
    normed, weights_b, picks = prepare(stash[...], route_cols, gain_row, router[...])
    normed_b[...] = normed
    both = (picks[0] + picks[1]).astype(BF16)
    picks_b[...] = both
    shifts[4].start()
    send_b[...] = to_slots(both, normed)
    send(1, send_b, rec_b)
    send_g[...] = to_slots(both, grad[...])
    send(2, send_g, rec_g)
    for k in range(4):
        shifts[k].start()
    p_row = jnp.sum(picks[0] * weights_b[0] + picks[1] * weights_b[1], 0, keepdims=True)
    halves = p_send.shape[0]
    for h in range(halves):
        p_send[h] = p_row[:, h * 128 : (h + 1) * 128]
    per_half = count // halves
    send(3, p_send, p_rec, lambda e: e // per_half)

    for m in range(3):
        to_twin(m).wait_recv()
        on_to_core(m).start()
    arrived(0, rec_a)
    rows[...] = flat(rec_a[...])
    for m in range(3):
        to_core(m).wait_recv()
        on_to_core(m).wait_recv()
        to_self(m).wait()
    acc[...] = jnp.zeros_like(acc)

    @pl.loop(0, quarters)
    def _(c):
        gate_val = dot_t(rows[...], gate[c])
        up_val = dot_t(rows[...], up[c])
        hidden = (gate_val * jax.nn.sigmoid(gate_val) * up_val).astype(BF16)
        acc[...] += dot(hidden, down[c])

    out_a[...] = acc[...].reshape(out_a.shape).astype(BF16)
    keep_back(4, out_a, back_a)
    send_back(4, out_a, back_a, 1, count // 2)
    arrived(1, rec_b)
    arrived(2, rec_g)
    arrived(3, p_rec)
    send_back(4, out_a, back_a, count // 2, count)

    rows[...] = flat(rec_b[...])
    grads[...] = flat(rec_g[...])
    acc[...] = jnp.zeros_like(acc)
    slots = count * MOST

    def back_part(c, dots):
        gate_val = dot_t(rows[...], gate[c])
        up_val = dot_t(rows[...], up[c])
        grad_hidden = dot_t(grads[...], down[c])
        sigma = jax.nn.sigmoid(gate_val)
        silu = gate_val * sigma
        hidden = (silu * up_val).astype(BF16)
        grad_gate = (grad_hidden * up_val * sigma * (1.0 + gate_val * (1.0 - sigma))).astype(BF16)
        grad_up = (grad_hidden * silu).astype(BF16)
        acc[...] += dot(grad_gate, gate[c]) + dot(grad_up, up[c])
        return dots + jnp.sum(hidden.astype(F32) * grad_hidden, -1, keepdims=True)

    dots = lax.fori_loop(0, quarters, back_part, jnp.zeros((slots, 1), F32))
    base = (me.expert() % per_half) * MOST
    lanes = ones(iota((count, MOST, 128), 2) == iota((count, MOST, 128), 1) + base)
    q_send[...] = jnp.sum(lanes * dots.reshape(count, MOST, 1), 1, keepdims=True)
    keep_back(5, q_send, q_back)
    send_back(5, q_send, q_back, 1, count)
    p_col = jnp.sum(lanes * p_rec[...], 2, keepdims=True).reshape(slots, 1)
    scaled = acc[...] * p_col
    out_b[...] = scaled.reshape(out_b.shape).astype(BF16)

    def grads_back(part):
        @pl.loop(part * count // 4, (part + 1) * count // 4)
        def _(j):
            device, slot = me.client(j)
            device = (behind, device[1], device[2])
            remote(out_b.at[slot], back_b.at[expert], ssem.at[6], rsem.at[6], device).start()

    grads_back(0)
    gain_own = jnp.sum(scaled * rows[...].astype(F32), 0, keepdims=True) / gain_row

    arrived(5, q_back)
    q_all = q_back[...]
    q_row = jnp.concatenate(
        [jnp.sum(q_all[h * per_half : (h + 1) * per_half], 0) for h in range(halves)], 1
    )
    dot_of = [jnp.sum(pick * q_row, -1, keepdims=True) for pick in picks]
    logit_grad = weights_b[0] * weights_b[1] * (dot_of[0] - dot_of[1])
    ids = iota((tokens, 128), 1)
    signs = ones(route_cols[0] == ids) - ones(route_cols[1] == ids)
    dlogits = (logit_grad * signs).astype(BF16)
    dlog[...] = dlogits
    shifts[5].start()
    x_float, inv_rms = norm_of(stash[...])
    dlogits = dlogits[:, :count]
    rsum[...] = dot(dlogits, normed_b[...], ((0,), (0,)))
    gain_part = gain_own + jnp.sum(dot(dlogits, router[...]) * x_float * inv_rms, 0, keepdims=True)
    per = count // group
    wide[...] = jnp.zeros_like(wide)
    for g in range(group):
        for c in range(ROWS_Z):
            wide[g, c, 0:per, :] = rsum[g * per : (g + 1) * per, c * 128 : (c + 1) * 128]
    for c in range(ROWS_Z):
        wide[0, c, per : per + 1, :] = gain_part[:, c * 128 : (c + 1) * 128]
    term[...] = wide[...].astype(BF16)

    @pl.loop(1, group)
    def _(o):
        other, device = in_row(o)
        remote(term.at[other], got.at[o - 1], sum_send.at[0], sum_recv.at[0], device).start()

    def summed(k, ref):
        return remote(ref, ref, sum_send.at[k], sum_recv.at[k], after)

    grads_back(1)
    summed(0, got).wait_recv()
    held[...] = (wide[mine] + jnp.sum(got[...].astype(F32), 0)).astype(BF16)

    @pl.loop(1, ROWS_Z)
    def _(o):
        other, device = in_column(o)
        remote(held.at[other], line.at[o - 1], sum_send.at[1], sum_recv.at[1], device).start()

    grads_back(2)
    summed(1, line).wait_recv()
    total[mine, me.z] = (held[me.z].astype(F32) + jnp.sum(line[...].astype(F32), 0)).astype(BF16)

    @pl.loop(1, ROWS_Z)
    def _(o):
        here = total.at[mine, me.z]
        remote(here, here, sum_send.at[2], sum_recv.at[2], in_column(o)[1]).start()

    grads_back(3)
    summed(2, line).wait_recv()

    @pl.loop(1, group)
    def _(o):
        remote(total.at[mine], total.at[mine], sum_send.at[3], sum_recv.at[3], in_row(o)[1]).start()

    arrived(4, back_a)
    returned = flat(back_a[...])
    mixed[...] = (
        act[...].astype(F32)
        + weights_a[0] * dot(picks_a[0].astype(BF16), returned)
        + weights_a[1] * dot(picks_a[1].astype(BF16), returned)
    ).astype(BF16)
    shifts[6].start()

    summed(3, got).wait_recv()
    scale = 1.0 / (group * ROWS_Z)
    wide[...] = total[...].astype(F32) * scale
    for g in range(group):
        for c in range(ROWS_Z):
            router_out[g * per : (g + 1) * per, c * 128 : (c + 1) * 128] = wide[g, c, 0:per, :]
    for c in range(ROWS_Z):
        gain_out[:, c * 128 : (c + 1) * 128] = wide[0, c, per : per + 1, :]

    for k in range(6):
        shifts[k].wait_recv()
    x_float, inv_rms = norm_of(stash_s[...])
    acc[0:tokens, :] = dot(dlog_s[...][:, :count], router_s[...])
    remote(out_b, back_b, ssem.at[6], rsem.at[6], after).wait_recv()
    dnormed = acc[0:tokens, :] + dot(picks_s[...], flat(back_b[...]))
    dxn = dnormed * gain_s[...]
    prev_grad[...] = (
        grad_s[...].astype(F32)
        + inv_rms * dxn
        - x_float * (inv_rms * inv_rms * inv_rms * jnp.mean(dxn * x_float, -1, keepdims=True))
    ).astype(BF16)

    for m in range(3):
        to_twin(m).wait_send()
        to_core(m).wait_send()
        on_to_core(m).wait_send()
    for k, ref in enumerate((rec_a, rec_b, rec_g, p_rec, back_a, q_back)):
        others(k, ref).wait_send()
    remote(out_b, back_b, ssem.at[6], rsem.at[6], after).wait_send()
    for k in range(7):
        shifts[k].wait_send()
    shifts[6].wait_recv()
    for k, ref in enumerate((got, line, line, got)):
        summed(k, ref).wait_send()


ANY = pl.BlockSpec(memory_space=pl.ANY)
VMEM = pl.BlockSpec(memory_space=pltpu.VMEM)


def like(shape, dtype):
    return jax.ShapeDtypeStruct(shape, dtype)


def body(
    act_in, stash_in, grad_in, route_a, route_b, norm_gain, router, gate_weight, up_weight, down_weight
):
    tokens, width = act_in.shape[1:]
    experts = router.shape[1]
    quarter = gate_weight.shape[2]
    group = lax.axis_size("expert") * lax.axis_size("dp") // ROWS_Z
    slots = experts * MOST
    block = (experts, MOST, width)
    dma = pltpu.SemaphoreType.DMA

    def vb(*shape):
        return pltpu.VMEM(shape, BF16)

    def vf(*shape):
        return pltpu.VMEM(shape, F32)

    full = vb(4, quarter, width)
    row = (tokens, width)
    lanes = (experts, 1, 128)
    next_act, prev_grad, router_grad, gain_grad = pl.pallas_call(
        kernel,
        out_shape=[like(row, BF16), like(row, BF16), like((experts, width), F32), like((1, width), F32)],
        in_specs=[VMEM] * 7 + [ANY] * 3,
        out_specs=[VMEM] * 4,
        scratch_shapes=[vb(*block)] * 6
        + [vb(slots, width)] * 2
        + [full] * 3
        + [vf(slots, width)]
        + [vb(*block)] * 4
        + [vb(*row)] * 2
        + [vb(*row)] * 2
        + [vb(tokens, slots)] * 2
        + [vb(experts, width), vf(1, width)]
        + [vb(tokens, 128)] * 2
        + [vf(slots // 128, 1, 128), vf(*lanes), vf(*lanes), vf(*lanes)]
        + [vf(experts, width), vf(group, ROWS_Z, 8, 128), vb(group, ROWS_Z, 8, 128), vb(ROWS_Z, 8, 128)]
        + [vb(group - 1, ROWS_Z, 8, 128), vb(ROWS_Z - 1, 8, 128), vb(group, ROWS_Z, 8, 128)]
        + [dma((7,)), dma((7,)), dma((6,)), dma((7,)), dma((7,))]
        + [dma((3, 3)), dma((3, 3)), dma((3,)), dma((4,)), dma((4,))],
        compiler_params=pltpu.CompilerParams(
            collective_id=0, has_side_effects=True, vmem_limit_bytes=56 << 20
        ),
    )(
        act_in[0], stash_in[0], grad_in[0], route_a[0].T, route_b[0].T, norm_gain, router[0],
        gate_weight[0, 0], up_weight[0, 0], down_weight[0, 0],
    )
    return next_act[None], prev_grad[None], router_grad[None], gain_grad


def solution(mesh):
    tokens = P("segment", ("expert", "dp"), None)
    weight = P("segment", "expert", "dp", None)
    router = P("segment", None, None)
    gain = P("segment", None)
    return jax.shard_map(
        body,
        mesh=mesh,
        in_specs=(tokens, tokens, tokens, tokens, tokens, gain, router, weight, weight, weight),
        out_specs=(tokens, tokens, router, gain),
        check_vma=False,
    )
```
